768 devices in a mesh: lat: 16 (over y, core), lon: 48 (over x, z).
Axes of the slice: x: 4, y: 8, z: 12, core: 2. Of those that a mesh axis runs over, the one named last changes fastest.
Arguments:
- features: bfloat16 [64, 256, 6144], P(None, 'lat', 'lon'), may hold values from -6 to 6
- labels: int32 [256, 6144], P('lat', 'lon'), may hold values from 0 to 5
- tile_regions: int32 [16, 48, 6], P('lat', 'lon'), may hold values from 0 to 5375, as said below
- bank_slot: int32 [5376], replicated, may hold values from 0 to 5375, as said below
- kernel_bank: bfloat16 [5376, 32, 512], P('lon'), may hold values from -0.25 to 0.25
- in_factor: bfloat16 [32, 64], replicated, may hold values from -0.75 to 0.75
- tap_factor: bfloat16 [16, 25], replicated, may hold values from -1.25 to 1.25
- out_factor: bfloat16 [64, 32], replicated, may hold values from -1 to 1
- out_bias: float32 [64], replicated, may hold values from -4 to 4
Outputs:
- mixed: bfloat16 [64, 256, 6144], P(None, 'lat', 'lon')
The draws below stay inside these ranges and needn't reach their ends.
Inputs may be any that keep to these rules, and one draw needn't show every extreme that they name: `tile_regions`: each tile lists 6 distinct regions: exactly 2 held by the bank device of its own lon index, 2 by that of the next lon index and 2 by that of the previous one (lon indices wrap); within one latitude band the tiles ask each bank device for exactly 4 distinct regions in all. A permutation: region r is bank row bank_slot[r], held by the lon device bank_slot[r] // 112.
All inputs are finite; a program needn't handle non-finite values.
Results may differ from the reference program's by a relative error of at most 0.0056.
Values may be sent and summed in bfloat16 or wider, within the bound.
A program may use at most 32 MiB of HBM per device.

```python
import jax
import jax.numpy as jnp
from jax import lax

CIN = 64
COUT = 64
RANK = 32
TAP_RANK = 16
KS = 5
TAPS = 25
REG_DEV = 112
REGIONS = 5376
CAP = 2
CAPU = 4
MAXR = 6
LAT_DEV = 16
LON_DEV = 128
NLAT = 256
NLON = 6144
N_LAT = 16
N_LON = 48


def slot_plan(key):
    return jax.random.permutation(jax.random.fold_in(key, 11), REGIONS).astype(jnp.int32)


def draw_bank_slot(key, part):
    return slot_plan(key)


def draw_tile_regions(key, part):
    slot_of = slot_plan(key)
    region_of = jnp.argsort(slot_of, stable=True).astype(jnp.int32)
    pool_keys = jax.random.split(jax.random.fold_in(key, 12), N_LAT * N_LON)
    pools = jax.vmap(lambda single: jax.random.permutation(single, REG_DEV)[:CAPU])(pool_keys)
    pools = pools.reshape(N_LAT, N_LON, CAPU).astype(jnp.int32)
    next_pools = jnp.roll(pools, -1, axis=1)
    prev_pools = jnp.roll(pools, 1, axis=1)
    first = jax.random.randint(jax.random.fold_in(key, 13), (N_LAT, N_LON), 0, CAPU)
    stride = jax.random.randint(jax.random.fold_in(key, 14), (N_LAT, N_LON), 1, CAPU)
    second = (first + stride) % CAPU
    pair = jnp.stack([first, second], axis=-1).astype(jnp.int32)
    from_prev = jnp.take_along_axis(prev_pools, pair, axis=-1)
    local_rows = jnp.concatenate([pools[:, :, :CAP], next_pools[:, :, CAP:2 * CAP], from_prev], axis=-1)
    strips = jnp.arange(N_LON, dtype=jnp.int32)[None, :, None]
    offsets = jnp.array([0, 0, 1, 1, -1, -1], dtype=jnp.int32)[None, None, :]
    owners = (strips + offsets + N_LON) % N_LON
    slots = owners * REG_DEV + local_rows
    regions = region_of[slots]
    order_keys = jax.random.split(jax.random.fold_in(key, 15), N_LAT * N_LON)
    orders = jax.vmap(lambda single: jax.random.permutation(single, MAXR))(order_keys).reshape(N_LAT, N_LON, MAXR)
    return jnp.take_along_axis(regions, orders.astype(jnp.int32), axis=-1).astype(jnp.int32)


def with_ends(drawn, rng, smallest, top_value):
    dims = drawn.shape
    spot = [jax.random.randint(jax.random.fold_in(rng, axis), (), 0, dims[axis]) for axis in range(len(dims))]
    drawn = drawn.at[tuple(spot)].set(smallest)
    longest = dims.index(max(dims))
    spot[longest] = (spot[longest] + 1) % dims[longest]
    return drawn.at[tuple(spot)].set(top_value)


def block_scale(stream_key, shape, shards, low, top_value):
    level, own = 1.0, jax.random.fold_in(stream_key, 6)
    for position, shards_of in shards:
        heights = jnp.exp(jax.random.uniform(jax.random.fold_in(own, position), (shards_of,), jnp.float32, low / len(shards), top_value / len(shards)))
        level = level * jnp.repeat(heights, shape[position] // shards_of).reshape([-1 if axis == position else 1 for axis in range(len(shape))])
    return level


def normal_values(rng, extent, scale, limit, cuts=(), held_as=jnp.bfloat16):
    result = scale * jax.random.normal(rng, extent, jnp.float32)
    if cuts:
        result = result * block_scale(rng, extent, cuts, -0.22, 0.18)
    return jnp.clip(result, -limit, limit).astype(held_as)


def setup_inputs(seed: int = 0) -> dict:
    splits = jax.random.split(jax.random.key(seed), 10)
    return {
        "features": normal_values(splits[0], (CIN, NLAT, NLON), 1.0, 6.0, ((1, 16), (2, 48))),
        "labels": with_ends(jax.random.randint(splits[1], (NLAT, NLON), 0, MAXR), jax.random.fold_in(splits[1], 1), 0, MAXR - 1).astype(jnp.int32),
        "tile_regions": draw_tile_regions(jax.random.fold_in(splits[9], 71), 0),
        "bank_slot": draw_bank_slot(jax.random.fold_in(splits[9], 71), 0),
        "kernel_bank": normal_values(splits[4], (REGIONS, RANK, TAP_RANK * RANK), (TAP_RANK * RANK) ** -0.5, 0.25, ((0, 48),)),
        "in_factor": normal_values(splits[5], (RANK, CIN), CIN ** -0.5, 0.75),
        "tap_factor": normal_values(splits[6], (TAP_RANK, TAPS), TAPS ** -0.5, 1.25),
        "out_factor": normal_values(splits[7], (COUT, RANK), RANK ** -0.5, 1.0),
        "out_bias": normal_values(splits[8], (COUT,), 1.0, 4.0, (), jnp.float32),
    }


def tile_layer(window, tile_labels, region_cores, tap_factor, out_factor, out_bias):
    lat_len = window.shape[1] - KS + 1
    lon_len = window.shape[2] - KS + 1
    shifted = [window[:, row_off:row_off + lat_len, col_off:col_off + lon_len] for row_off in range(KS) for col_off in range(KS)]
    stacked = jnp.stack(shifted).reshape(KS * KS, -1)
    tapped = jnp.dot(tap_factor, stacked, preferred_element_type=jnp.float32).astype(jnp.bfloat16)
    tapped = tapped.reshape(-1, lat_len * lon_len)
    tucker_rank = region_cores.shape[1]
    list_len = region_cores.shape[0]
    flat_cores = region_cores.reshape(list_len * tucker_rank, -1)
    all_regions = jnp.dot(flat_cores, tapped, preferred_element_type=jnp.float32).reshape(list_len, tucker_rank, -1)
    onehot = (tile_labels.reshape(-1)[None, :] == jnp.arange(list_len, dtype=jnp.int32)[:, None]).astype(jnp.float32)
    hidden = jnp.sum(all_regions * onehot[:, None, :], axis=0).astype(jnp.bfloat16)
    output = jnp.dot(out_factor, hidden, preferred_element_type=jnp.float32) + out_bias[:, None]
    return jax.nn.silu(output).astype(jnp.bfloat16).reshape(-1, lat_len, lon_len)


def reference(features, labels, tile_regions, bank_slot, kernel_bank, in_factor, tap_factor, out_factor, out_bias):
    reach = KS // 2
    flat = features.reshape(CIN, -1)
    reduced = jnp.dot(in_factor, flat, preferred_element_type=jnp.float32).astype(jnp.bfloat16).reshape(RANK, NLAT, NLON)
    widened = jnp.concatenate([reduced[:, :, NLON - reach:], reduced, reduced[:, :, :reach]], axis=2)
    padded = jnp.pad(widened, ((0, 0), (reach, reach), (0, 0)))

    def one_tile(tile_index):
        band = (tile_index // N_LON).astype(jnp.int32)
        strip = (tile_index % N_LON).astype(jnp.int32)
        window = lax.dynamic_slice(padded, (jnp.int32(0), band * LAT_DEV, strip * LON_DEV), (RANK, LAT_DEV + 2 * reach, LON_DEV + 2 * reach))
        tile_labels = lax.dynamic_slice(labels, (band * LAT_DEV, strip * LON_DEV), (LAT_DEV, LON_DEV))
        region_cores = kernel_bank[bank_slot[tile_regions[band, strip]]]
        return tile_layer(window, tile_labels, region_cores, tap_factor, out_factor, out_bias)

    tiles = lax.map(one_tile, jnp.arange(N_LAT * N_LON, dtype=jnp.int32))
    tiles = tiles.reshape(N_LAT, N_LON, COUT, LAT_DEV, LON_DEV)
    return tiles.transpose(2, 0, 3, 1, 4).reshape(COUT, NLAT, NLON)
```

```python
import functools

import jax
import jax.numpy as jnp
from jax import lax
from jax.experimental import pallas as pl
from jax.experimental.pallas import tpu as pltpu
from jax.sharding import PartitionSpec as P

KS = 5
REACH = KS // 2
LANES = 128
MAXR = 6
BF16 = jnp.bfloat16
F32 = jnp.float32
MESH = pl.DeviceIdType.MESH


def dot(a, b):
    return jnp.dot(a, b, preferred_element_type=F32)


def kernel(
    n_lat, n_lon,
    feat_h, lab_h, tr_h, slot_h, bank_h, inf_h, tap_h, outf_h, bias_h,
    out_ref,
    feat_v, lab_v, tr_s, slot_s, bank_v, inf_v, tap_v, outf_v, bias_v,
    ask_s, asked_s, spread, red, pack, packs, tops, bots, send_cores, cores,
    kron, moved, tapped, held, local_sem, send_sem, recv_sem,
):
    lat, lon = lax.axis_index("lat"), lax.axis_index("lon")
    up, down = lax.rem(lat + (n_lat - 1), n_lat), lax.rem(lat + 1, n_lat)
    prev, nxt = lax.rem(lon + (n_lon - 1), n_lon), lax.rem(lon + 1, n_lon)
    channels, rows, _ = feat_v.shape
    rank = inf_v.shape[0]
    taps_rank = tap_v.shape[0]
    bank_rows = bank_v.shape[0]
    around = [(lat, prev), (lat, nxt), (up, lon), (down, lon), (up, prev), (up, nxt), (down, prev), (down, nxt)]

    barrier = pltpu.get_barrier_semaphore()
    for place in around:
        pl.semaphore_signal(barrier, inc=1, device_id=place, device_id_type=MESH)

    def local(source, target, index):
        copy = pltpu.make_async_copy(source, target, local_sem.at[index])
        copy.start()
        return copy

    get_tr = local(tr_h, tr_s, 0)
    get_slot = local(slot_h, slot_s, 1)
    get_feat = local(feat_h, feat_v, 2)
    get_inf = local(inf_h, inf_v, 3)
    get_tap = local(tap_h, tap_v, 4)
    get_lab = local(lab_h, lab_v, 5)
    get_outf = local(outf_h, outf_v, 6)
    get_bias = local(bias_h, bias_v, 7)
    part = bank_rows // 4
    get_bank = [
        local(bank_h.at[pl.ds(i * part, part)], bank_v.at[pl.ds(i * part, part)], 8 + i) for i in range(4)
    ]

    def remote(source, target, index, place):
        return pltpu.make_async_remote_copy(
            src_ref=source, dst_ref=target, send_sem=send_sem.at[index], recv_sem=recv_sem.at[index],
            device_id=place, device_id_type=MESH,
        )

    get_tr.wait()
    get_slot.wait()
    slots = [slot_s[tr_s[0, 0, j]] for j in range(MAXR)]

    def wanted(owner):
        first = owner * bank_rows
        row_a = row_b = at_a = at_b = count = jnp.int32(0)
        for j in range(MAXR):
            row = slots[j] - first
            hit = (row >= 0) & (row < bank_rows)
            is_a = hit & (count == 0)
            is_b = hit & (count == 1)
            row_a, at_a = jnp.where(is_a, row, row_a), jnp.where(is_a, j, at_a)
            row_b, at_b = jnp.where(is_b, row, row_b), jnp.where(is_b, j, at_b)
            count = count + hit.astype(jnp.int32)
        return row_a, row_b, at_a, at_b

    own_a, own_b, own_at, _ = wanted(lon)
    prev_a, prev_b, prev_at_a, prev_at_b = wanted(prev)
    next_a, next_b, next_at_a, next_at_b = wanted(nxt)
    ask_s[0, 0], ask_s[0, 1] = prev_a, prev_b
    ask_s[1, 0], ask_s[1, 1] = next_a, next_b

    pl.semaphore_wait(barrier, len(around))
    ask_prev = remote(ask_s.at[0], asked_s.at[1], 0, (lat, prev))
    ask_next = remote(ask_s.at[1], asked_s.at[0], 1, (lat, nxt))
    ask_prev.start()
    ask_next.start()

    get_feat.wait()
    get_inf.wait()
    spread[...] = feat_v[...].astype(F32).reshape(channels * rows, LANES)
    lane = lax.broadcasted_iota(jnp.int32, (rank, LANES), 1)
    packed = jnp.zeros((rank, LANES), F32)
    weights = inf_v[...]
    for r in range(rows):
        columns = spread[pl.ds(r, channels, stride=rows), :].astype(BF16)
        block = dot(weights, columns).astype(BF16)
        red[:, r * LANES : (r + 1) * LANES] = block
        rolled = pltpu.roll(block.astype(F32), (4 * r + 2) % LANES, 1)
        packed = jnp.where((lane >= 4 * r) & (lane < 4 * r + 4), rolled, packed)
    pack[...] = packed.astype(BF16)

    edge = REACH * LANES
    whole = rows * LANES
    rims = [
        remote(pack, packs.at[1], 2, (lat, prev)),
        remote(pack, packs.at[0], 3, (lat, nxt)),
        remote(red.at[:, pl.ds(0, edge)], bots, 4, (up, lon)),
        remote(red.at[:, pl.ds(whole - edge, edge)], tops, 5, (down, lon)),
        remote(pack, packs.at[5], 6, (up, prev)),
        remote(pack, packs.at[4], 7, (up, nxt)),
        remote(pack, packs.at[3], 8, (down, prev)),
        remote(pack, packs.at[2], 9, (down, nxt)),
    ]
    for copy in rims:
        copy.start()

    for copy in get_bank:
        copy.wait()
    ask_prev.wait_recv()
    send_cores[0] = bank_v[asked_s[1, 0]]
    send_cores[1] = bank_v[asked_s[1, 1]]
    ask_next.wait_recv()
    send_cores[2] = bank_v[asked_s[0, 0]]
    send_cores[3] = bank_v[asked_s[0, 1]]
    give_next = remote(send_cores.at[pl.ds(0, 2)], cores.at[pl.ds(0, 2)], 10, (lat, nxt))
    give_prev = remote(send_cores.at[pl.ds(2, 2)], cores.at[pl.ds(2, 2)], 11, (lat, prev))
    give_next.start()
    give_prev.start()

    get_tap.wait()
    depth = kron.shape[1]
    taps = tap_v.shape[1]
    pick = (
        lax.broadcasted_iota(jnp.int32, (taps, depth), 1) // rank == lax.broadcasted_iota(jnp.int32, (taps, depth), 0)
    ).astype(F32).astype(BF16)
    wide = dot(tap_v[...], pick)
    same = lax.broadcasted_iota(jnp.int32, (rank, depth), 1) % rank == lax.broadcasted_iota(jnp.int32, (rank, depth), 0)
    for c in range(taps_rank):
        kron[c * rank : (c + 1) * rank, :] = jnp.where(
            same, jnp.broadcast_to(wide[c : c + 1, :], (rank, depth)), 0.0
        ).astype(BF16)

    for copy in rims:
        copy.wait_recv()
    not_first = (lat > 0).astype(F32)
    not_last = (lat < n_lat - 1).astype(F32)
    even = lane % 4 < 2

    def place_row(at, block, sides, row):
        beside = pltpu.roll(sides, (LANES - 2 - 4 * row) % LANES, 1)
        shapes = (
            pltpu.roll(jnp.where(lane >= LANES - 2, beside, block), 2, 1),
            pltpu.roll(jnp.where(lane == LANES - 1, beside, block), 1, 1),
            block,
            pltpu.roll(jnp.where(lane == 0, beside, block), LANES - 1, 1),
            pltpu.roll(jnp.where(lane < 2, beside, block), LANES - 2, 1),
        )
        for dx in range(KS):
            moved[dx * rank : (dx + 1) * rank, at * LANES : (at + 1) * LANES] = shapes[dx].astype(BF16)

    middle = jnp.where(even, packs[0].astype(F32), packs[1].astype(F32))
    above = jnp.where(even, packs[2].astype(F32), packs[3].astype(F32)) * not_first
    below = jnp.where(even, packs[4].astype(F32), packs[5].astype(F32)) * not_last
    for r in range(REACH):
        lanes = pl.ds(r * LANES, LANES)
        place_row(r, tops[:, lanes].astype(F32) * not_first, above, rows - REACH + r)
        place_row(rows + REACH + r, bots[:, lanes].astype(F32) * not_last, below, r)
    for r in range(rows):
        place_row(REACH + r, red[:, r * LANES : (r + 1) * LANES].astype(F32), middle, r)

    get_lab.wait()
    own_cores = jnp.concatenate([bank_v[own_a], bank_v[own_b]], axis=0)
    span = 2 * LANES

    def label_of(i):
        return jnp.concatenate(
            [jnp.broadcast_to(lab_v[pl.ds(2 * i + k, 1), :], (rank, LANES)) for k in range(2)], axis=1
        )

    @pl.loop(0, rows // 2)
    def _(i):
        start = pl.multiple_of(i * span, span)
        pieces = [moved[:, pl.ds(pl.multiple_of(start + dy * LANES, LANES), span)] for dy in range(KS)]
        pieces.append(jnp.zeros((depth - KS * KS * rank, span), BF16))
        result = dot(kron[...], jnp.concatenate(pieces, axis=0)).astype(BF16)
        tapped[:, pl.ds(start, span)] = result
        ours = dot(own_cores, result)
        held[:, pl.ds(start, span)] = jnp.where(label_of(i) == own_at, ours[:rank], ours[rank:])

    get_outf.wait()
    get_bias.wait()
    square = (channels, channels)
    eye = lax.broadcasted_iota(jnp.int32, square, 0) == lax.broadcasted_iota(jnp.int32, square, 1)
    bias = jnp.sum(jnp.where(eye, jnp.broadcast_to(bias_v[...], square), 0.0), axis=1, keepdims=True)
    give_next.wait_recv()
    give_prev.wait_recv()
    others = cores[...].reshape(4 * rank, cores.shape[2])
    last = outf_v[...]

    @pl.loop(0, rows // 2)
    def _(i):
        start = pl.multiple_of(i * span, span)
        theirs = dot(others, tapped[:, pl.ds(start, span)])
        label = label_of(i)
        hidden = held[:, pl.ds(start, span)]
        for k, at in enumerate((prev_at_a, prev_at_b, next_at_a, next_at_b)):
            hidden = jnp.where(label == at, theirs[k * rank : (k + 1) * rank], hidden)
        value = dot(last, hidden.astype(BF16)) + bias
        value = value / (1.0 + jnp.exp(-value))
        for k in range(2):
            spread[pl.ds(2 * i + k, channels, stride=rows), :] = value[:, k * LANES : (k + 1) * LANES]

    out_ref[...] = spread[...].reshape(channels, rows, LANES).astype(BF16)

    ask_prev.wait_send()
    ask_next.wait_send()
    for copy in rims:
        copy.wait_send()
    give_next.wait_send()
    give_prev.wait_send()


def on_device(features, labels, tile_regions, bank_slot, kernel_bank, in_factor, tap_factor, out_factor, out_bias):
    n_lat, n_lon = lax.axis_size("lat"), lax.axis_size("lon")
    channels, rows, columns = features.shape
    rank = in_factor.shape[0]
    taps_rank, taps = tap_factor.shape
    bank_rows, _, width = kernel_bank.shape
    depth = -(-taps * rank // LANES) * LANES
    cells = rows * columns
    wide = (rows + 2 * REACH) * columns
    dma = pltpu.SemaphoreType.DMA
    anywhere = pl.BlockSpec(memory_space=pltpu.HBM)
    return pl.pallas_call(
        functools.partial(kernel, n_lat, n_lon),
        out_shape=jax.ShapeDtypeStruct(features.shape, BF16),
        in_specs=[anywhere] * 9,
        out_specs=pl.BlockSpec(memory_space=pltpu.VMEM),
        scratch_shapes=[
            pltpu.VMEM(features.shape, BF16),
            pltpu.VMEM(labels.shape, jnp.int32),
            pltpu.SMEM(tile_regions.shape, jnp.int32),
            pltpu.SMEM(bank_slot.shape, jnp.int32),
            pltpu.VMEM(kernel_bank.shape, BF16),
            pltpu.VMEM(in_factor.shape, BF16),
            pltpu.VMEM(tap_factor.shape, BF16),
            pltpu.VMEM(out_factor.shape, BF16),
            pltpu.VMEM((1, out_bias.shape[0]), F32),
            pltpu.SMEM((2, 2), jnp.int32),
            pltpu.SMEM((2, 2), jnp.int32),
            pltpu.VMEM((channels * rows, columns), F32),
            pltpu.VMEM((rank, cells), BF16),
            pltpu.VMEM((rank, columns), BF16),
            pltpu.VMEM((6, rank, columns), BF16),
            pltpu.VMEM((rank, REACH * columns), BF16),
            pltpu.VMEM((rank, REACH * columns), BF16),
            pltpu.VMEM((4, rank, width), BF16),
            pltpu.VMEM((4, rank, width), BF16),
            pltpu.VMEM((taps_rank * rank, depth), BF16),
            pltpu.VMEM((KS * rank, wide), BF16),
            pltpu.VMEM((taps_rank * rank, cells), BF16),
            pltpu.VMEM((rank, cells), F32),
            dma((12,)),
            dma((12,)),
            dma((12,)),
        ],
        compiler_params=pltpu.CompilerParams(
            collective_id=0, has_side_effects=True, vmem_limit_bytes=48 * 1024 * 1024
        ),
        name="layer",
    )(
        features, labels, tile_regions, bank_slot, kernel_bank, in_factor, tap_factor, out_factor,
        out_bias.reshape(1, -1),
    )


def solution(mesh):
    placed = (
        P(None, "lat", "lon"),
        P("lat", "lon"),
        P("lat", "lon", None),
        P(),
        P("lon", None, None),
        P(),
        P(),
        P(),
        P(),
    )
    return jax.shard_map(
        on_device, mesh=mesh, in_specs=placed, out_specs=P(None, "lat", "lon"), check_vma=False
    )
```

```python
import functools

import jax
import jax.numpy as jnp
from jax import lax
from jax.experimental import pallas as pl
from jax.experimental.pallas import tpu as pltpu
from jax.sharding import PartitionSpec as P

KS = 5
REACH = KS // 2
LANES = 128
MAXR = 6
WAVE = 12
BF16 = jnp.bfloat16
F32 = jnp.float32
MESH = pl.DeviceIdType.MESH


def dot(a, b):
    return jnp.dot(a, b, preferred_element_type=F32)


def kernel(
    n_lat, n_lon,
    feat_h, lab_h, tr_h, slot_h, bank_h, inf_h, tap_h, outf_h, bias_h,
    out_ref,
    feat_v, lab_v, tr_s, slot_s, bank_v, inf_v, tap_v, outf_v, bias_v,
    ask_s, asked_s, spread, red, pack, packs, tops, bots, send_cores, cores,
    kron, moved, tapped, held, local_sem, send_sem, recv_sem, hello,
):
    lat, lon = lax.axis_index("lat"), lax.axis_index("lon")
    up, down = lax.rem(lat + (n_lat - 1), n_lat), lax.rem(lat + 1, n_lat)
    prev, nxt = lax.rem(lon + (n_lon - 1), n_lon), lax.rem(lon + 1, n_lon)
    channels, rows, _ = feat_v.shape
    rank = inf_v.shape[0]
    taps_rank = tap_v.shape[0]
    bank_rows = bank_v.shape[0]
    z = lax.rem(lon, WAVE)
    head, tail, odd = z == 0, z == WAVE - 1, lax.rem(lat, 2) == 1
    even_lat = lax.rem(lat, 2) == 0
    barrier = pltpu.get_barrier_semaphore()

    def signal(semaphore, place):
        pl.semaphore_signal(semaphore, inc=1, device_id=place, device_id_type=MESH)

    @pl.when(z != WAVE - 1)
    def _():
        for line in (lat, up, down):
            signal(barrier, (line, nxt))

    @pl.when(head)
    def _():
        for line in (lat, up, down):
            signal(barrier, (line, prev))

    @pl.when(odd)
    def _():
        for line in (up, down):
            signal(barrier, (line, lon))

    def local(source, target, index):
        copy = pltpu.make_async_copy(source, target, local_sem.at[index])
        copy.start()
        return copy

    get_tr = local(tr_h, tr_s, 0)
    get_slot = local(slot_h, slot_s, 1)
    get_feat = local(feat_h, feat_v, 2)
    get_inf = local(inf_h, inf_v, 3)
    get_tap = local(tap_h, tap_v, 4)
    get_lab = local(lab_h, lab_v, 5)
    get_outf = local(outf_h, outf_v, 6)
    get_bias = local(bias_h, bias_v, 7)
    part = bank_rows // 4
    get_bank = [
        local(bank_h.at[pl.ds(i * part, part)], bank_v.at[pl.ds(i * part, part)], 8 + i) for i in range(4)
    ]

    def remote(source, target, index, place):
        return pltpu.make_async_remote_copy(
            src_ref=source, dst_ref=target, send_sem=send_sem.at[index], recv_sem=recv_sem.at[index],
            device_id=place, device_id_type=MESH,
        )

    count = jnp.where(head, 0, 3) + jnp.where(tail, 3, 0) + jnp.where(odd, 0, 2)

    @pl.when(count > 0)
    def _():
        pl.semaphore_wait(barrier, count)

    @pl.when(z != 0)
    def _():
        signal(hello.at[1], (lat, prev))
        signal(hello.at[7], (up, prev))
        signal(hello.at[5], (down, prev))

    @pl.when(tail)
    def _():
        signal(hello.at[0], (lat, nxt))
        signal(hello.at[6], (up, nxt))
        signal(hello.at[4], (down, nxt))

    @pl.when(even_lat)
    def _():
        signal(hello.at[3], (up, lon))
        signal(hello.at[2], (down, lon))

    def heard(*indices):
        for index in indices:
            pl.semaphore_wait(hello.at[index], 1)

    get_tr.wait()
    get_slot.wait()
    slots = [slot_s[tr_s[0, 0, j]] for j in range(MAXR)]

    def wanted(owner):
        first = owner * bank_rows
        row_a = row_b = at_a = at_b = count = jnp.int32(0)
        for j in range(MAXR):
            row = slots[j] - first
            hit = (row >= 0) & (row < bank_rows)
            is_a = hit & (count == 0)
            is_b = hit & (count == 1)
            row_a, at_a = jnp.where(is_a, row, row_a), jnp.where(is_a, j, at_a)
            row_b, at_b = jnp.where(is_b, row, row_b), jnp.where(is_b, j, at_b)
            count = count + hit.astype(jnp.int32)
        return row_a, row_b, at_a, at_b

    own_a, own_b, own_at, _ = wanted(lon)
    prev_a, prev_b, prev_at_a, prev_at_b = wanted(prev)
    next_a, next_b, next_at_a, next_at_b = wanted(nxt)
    ask_s[0, 0], ask_s[0, 1] = prev_a, prev_b
    ask_s[1, 0], ask_s[1, 1] = next_a, next_b

    ask_prev = remote(ask_s.at[0], asked_s.at[1], 0, (lat, prev))
    ask_next = remote(ask_s.at[1], asked_s.at[0], 1, (lat, nxt))

    @pl.when(z != 0)
    def _():
        ask_prev.start()

    @pl.when(z != WAVE - 1)
    def _():
        heard(1)

    ask_next.start()

    get_feat.wait()
    get_inf.wait()
    spread[...] = feat_v[...].astype(F32).reshape(channels * rows, LANES)
    lane = lax.broadcasted_iota(jnp.int32, (rank, LANES), 1)
    packed = jnp.zeros((rank, LANES), F32)
    weights = inf_v[...]
    for r in range(rows):
        columns = spread[pl.ds(r, channels, stride=rows), :].astype(BF16)
        block = dot(weights, columns).astype(BF16)
        red[:, r * LANES : (r + 1) * LANES] = block
        rolled = pltpu.roll(block.astype(F32), (4 * r + 2) % LANES, 1)
        packed = jnp.where((lane >= 4 * r) & (lane < 4 * r + 4), rolled, packed)
    pack[...] = packed.astype(BF16)

    edge = REACH * LANES
    whole = rows * LANES
    rims_prev = [
        remote(pack, packs.at[1], 2, (lat, prev)),
        remote(pack, packs.at[5], 6, (up, prev)),
        remote(pack, packs.at[3], 8, (down, prev)),
    ]
    rims_next = [
        remote(pack, packs.at[0], 3, (lat, nxt)),
        remote(pack, packs.at[4], 7, (up, nxt)),
        remote(pack, packs.at[2], 9, (down, nxt)),
    ]
    rims_lat = [
        remote(red.at[:, pl.ds(0, edge)], bots, 4, (up, lon)),
        remote(red.at[:, pl.ds(whole - edge, edge)], tops, 5, (down, lon)),
    ]
    rims = rims_prev + rims_next + rims_lat

    @pl.when(z != WAVE - 1)
    def _():
        heard(5, 7)

    for copy in rims_next:
        copy.start()

    @pl.when(z != 0)
    def _():
        for copy in rims_prev:
            copy.start()

    @pl.when(odd)
    def _():
        heard(2, 3)

    for copy in rims_lat:
        copy.start()

    give_next = remote(send_cores.at[pl.ds(0, 2)], cores.at[pl.ds(0, 2)], 10, (lat, nxt))
    give_prev = remote(send_cores.at[pl.ds(2, 2)], cores.at[pl.ds(2, 2)], 11, (lat, prev))

    def serve_next():
        ask_prev.wait_recv()
        send_cores[0] = bank_v[asked_s[1, 0]]
        send_cores[1] = bank_v[asked_s[1, 1]]
        give_next.start()

    def serve_prev():
        ask_next.wait_recv()
        send_cores[2] = bank_v[asked_s[0, 0]]
        send_cores[3] = bank_v[asked_s[0, 1]]
        give_prev.start()

    for copy in get_bank:
        copy.wait()
    serve_next()
    pl.when(z != 0)(serve_prev)

    get_tap.wait()
    depth = kron.shape[1]
    taps = tap_v.shape[1]
    pick = (
        lax.broadcasted_iota(jnp.int32, (taps, depth), 1) // rank == lax.broadcasted_iota(jnp.int32, (taps, depth), 0)
    ).astype(F32).astype(BF16)
    wide = dot(tap_v[...], pick)
    same = lax.broadcasted_iota(jnp.int32, (rank, depth), 1) % rank == lax.broadcasted_iota(jnp.int32, (rank, depth), 0)
    for c in range(taps_rank):
        kron[c * rank : (c + 1) * rank, :] = jnp.where(
            same, jnp.broadcast_to(wide[c : c + 1, :], (rank, depth)), 0.0
        ).astype(BF16)

    @pl.when(head)
    def _():
        heard(0)
        ask_prev.start()
        heard(4, 6)
        for copy in rims_prev:
            copy.start()
        serve_prev()

    for copy in rims:
        copy.wait_recv()
    not_first = (lat > 0).astype(F32)
    not_last = (lat < n_lat - 1).astype(F32)
    even = lane % 4 < 2

    def place_row(at, block, sides, row):
        beside = pltpu.roll(sides, (LANES - 2 - 4 * row) % LANES, 1)
        shapes = (
            pltpu.roll(jnp.where(lane >= LANES - 2, beside, block), 2, 1),
            pltpu.roll(jnp.where(lane == LANES - 1, beside, block), 1, 1),
            block,
            pltpu.roll(jnp.where(lane == 0, beside, block), LANES - 1, 1),
            pltpu.roll(jnp.where(lane < 2, beside, block), LANES - 2, 1),
        )
        for dx in range(KS):
            moved[dx * rank : (dx + 1) * rank, at * LANES : (at + 1) * LANES] = shapes[dx].astype(BF16)

    middle = jnp.where(even, packs[0].astype(F32), packs[1].astype(F32))
    above = jnp.where(even, packs[2].astype(F32), packs[3].astype(F32)) * not_first
    below = jnp.where(even, packs[4].astype(F32), packs[5].astype(F32)) * not_last
    for r in range(REACH):
        lanes = pl.ds(r * LANES, LANES)
        place_row(r, tops[:, lanes].astype(F32) * not_first, above, rows - REACH + r)
        place_row(rows + REACH + r, bots[:, lanes].astype(F32) * not_last, below, r)
    for r in range(rows):
        place_row(REACH + r, red[:, r * LANES : (r + 1) * LANES].astype(F32), middle, r)

    get_lab.wait()
    own_cores = jnp.concatenate([bank_v[own_a], bank_v[own_b]], axis=0)
    span = 2 * LANES

    def label_of(i):
        return jnp.concatenate(
            [jnp.broadcast_to(lab_v[pl.ds(2 * i + k, 1), :], (rank, LANES)) for k in range(2)], axis=1
        )

    @pl.loop(0, rows // 2)
    def _(i):
        start = pl.multiple_of(i * span, span)
        pieces = [moved[:, pl.ds(pl.multiple_of(start + dy * LANES, LANES), span)] for dy in range(KS)]
        pieces.append(jnp.zeros((depth - KS * KS * rank, span), BF16))
        result = dot(kron[...], jnp.concatenate(pieces, axis=0)).astype(BF16)
        tapped[:, pl.ds(start, span)] = result
        ours = dot(own_cores, result)
        held[:, pl.ds(start, span)] = jnp.where(label_of(i) == own_at, ours[:rank], ours[rank:])

    get_outf.wait()
    get_bias.wait()
    square = (channels, channels)
    eye = lax.broadcasted_iota(jnp.int32, square, 0) == lax.broadcasted_iota(jnp.int32, square, 1)
    bias = jnp.sum(jnp.where(eye, jnp.broadcast_to(bias_v[...], square), 0.0), axis=1, keepdims=True)
    give_next.wait_recv()
    give_prev.wait_recv()
    others = cores[...].reshape(4 * rank, cores.shape[2])
    last = outf_v[...]

    @pl.loop(0, rows // 2)
    def _(i):
        start = pl.multiple_of(i * span, span)
        theirs = dot(others, tapped[:, pl.ds(start, span)])
        label = label_of(i)
        hidden = held[:, pl.ds(start, span)]
        for k, at in enumerate((prev_at_a, prev_at_b, next_at_a, next_at_b)):
            hidden = jnp.where(label == at, theirs[k * rank : (k + 1) * rank], hidden)
        value = lax.dot_general(last, hidden.astype(BF16), (((0,), (0,)), ((), ())), preferred_element_type=F32) + bias
        value = value / (1.0 + jnp.exp(-value))
        for k in range(2):
            spread[pl.ds(2 * i + k, channels, stride=rows), :] = value[:, k * LANES : (k + 1) * LANES]

    out_ref[...] = spread[...].reshape(channels, rows, LANES).astype(BF16)

    ask_prev.wait_send()
    ask_next.wait_send()
    for copy in rims:
        copy.wait_send()
    give_next.wait_send()
    give_prev.wait_send()


def on_device(features, labels, tile_regions, bank_slot, kernel_bank, in_factor, tap_factor, out_factor, out_bias):
    n_lat, n_lon = lax.axis_size("lat"), lax.axis_size("lon")
    channels, rows, columns = features.shape
    rank = in_factor.shape[0]
    taps_rank, taps = tap_factor.shape
    bank_rows, _, width = kernel_bank.shape
    depth = -(-taps * rank // LANES) * LANES
    cells = rows * columns
    wide = (rows + 2 * REACH) * columns
    dma = pltpu.SemaphoreType.DMA
    anywhere = pl.BlockSpec(memory_space=pltpu.HBM)
    return pl.pallas_call(
        functools.partial(kernel, n_lat, n_lon),
        out_shape=pltpu.VMEM(features.shape, BF16),
        in_specs=[anywhere] * 9,
        out_specs=pl.BlockSpec(memory_space=pltpu.VMEM),
        scratch_shapes=[
            pltpu.VMEM(features.shape, BF16),
            pltpu.VMEM(labels.shape, jnp.int32),
            pltpu.SMEM(tile_regions.shape, jnp.int32),
            pltpu.SMEM(bank_slot.shape, jnp.int32),
            pltpu.VMEM(kernel_bank.shape, BF16),
            pltpu.VMEM(in_factor.shape, BF16),
            pltpu.VMEM(tap_factor.shape, BF16),
            pltpu.VMEM(out_factor.shape[::-1], BF16),
            pltpu.VMEM((1, out_bias.shape[0]), F32),
            pltpu.SMEM((2, 2), jnp.int32),
            pltpu.SMEM((2, 2), jnp.int32),
            pltpu.VMEM((channels * rows, columns), F32),
            pltpu.VMEM((rank, cells), BF16),
            pltpu.VMEM((rank, columns), BF16),
            pltpu.VMEM((6, rank, columns), BF16),
            pltpu.VMEM((rank, REACH * columns), BF16),
            pltpu.VMEM((rank, REACH * columns), BF16),
            pltpu.VMEM((4, rank, width), BF16),
            pltpu.VMEM((4, rank, width), BF16),
            pltpu.VMEM((taps_rank * rank, depth), BF16),
            pltpu.VMEM((KS * rank, wide), BF16),
            pltpu.VMEM((taps_rank * rank, cells), BF16),
            pltpu.VMEM((rank, cells), F32),
            dma((12,)),
            dma((12,)),
            dma((12,)),
            pltpu.SemaphoreType.REGULAR((8,)),
        ],
        compiler_params=pltpu.CompilerParams(
            collective_id=0, has_side_effects=True, vmem_limit_bytes=56 * 1024 * 1024
        ),
        name="layer",
    )(
        features, labels, tile_regions, bank_slot, kernel_bank, in_factor, tap_factor, out_factor.T,
        out_bias.reshape(1, -1),
    )


def solution(mesh):
    placed = (
        P(None, "lat", "lon"),
        P("lat", "lon"),
        P("lat", "lon", None),
        P(),
        P("lon", None, None),
        P(),
        P(),
        P(),
        P(),
    )
    return jax.shard_map(
        on_device, mesh=mesh, in_specs=placed, out_specs=P(None, "lat", "lon"), check_vma=False
    )
```

```python
import functools

import jax
import jax.numpy as jnp
from jax import lax
from jax.experimental import pallas as pl
from jax.experimental.pallas import tpu as pltpu
from jax.sharding import PartitionSpec as P

KS = 5
REACH = KS // 2
LANES = 128
MAXR = 6
WAVE = 12
BF16 = jnp.bfloat16
F32 = jnp.float32
MESH = pl.DeviceIdType.MESH


def dot(a, b):
    return jnp.dot(a, b, preferred_element_type=F32)


def kernel(
    n_lat, n_lon,
    feat_h, lab_h, tr_h, slot_h, bank_h, inf_h, tap_h, outf_h, bias_h,
    out_ref,
    feat_v, lab_v, tr_s, slot_s, bank_v, inf_v, tap_v, outf_v, bias_v,
    ask_s, asked_s, spread, red, pack, packs, tops, bots, send_cores, cores,
    kron, moved, rim_cells, tapped, held, local_sem, send_sem, recv_sem, hello,
):
    lat, lon = lax.axis_index("lat"), lax.axis_index("lon")
    up, down = lax.rem(lat + (n_lat - 1), n_lat), lax.rem(lat + 1, n_lat)
    prev, nxt = lax.rem(lon + (n_lon - 1), n_lon), lax.rem(lon + 1, n_lon)
    channels, rows, _ = feat_v.shape
    rank = inf_v.shape[0]
    taps_rank = tap_v.shape[0]
    bank_rows = bank_v.shape[0]
    z = lax.rem(lon, WAVE)
    head, tail, odd = z == 0, z == WAVE - 1, lax.rem(lat, 2) == 1
    even_lat = lax.rem(lat, 2) == 0
    barrier = pltpu.get_barrier_semaphore()

    def signal(semaphore, place):
        pl.semaphore_signal(semaphore, inc=1, device_id=place, device_id_type=MESH)

    @pl.when(z != WAVE - 1)
    def _():
        for line in (lat, up, down):
            signal(barrier, (line, nxt))

    @pl.when(head)
    def _():
        for line in (lat, up, down):
            signal(barrier, (line, prev))

    @pl.when(odd)
    def _():
        for line in (up, down):
            signal(barrier, (line, lon))

    def local(source, target, index):
        copy = pltpu.make_async_copy(source, target, local_sem.at[index])
        copy.start()
        return copy

    get_tr = local(tr_h, tr_s, 0)
    get_slot = local(slot_h, slot_s, 1)
    get_feat = local(feat_h, feat_v, 2)
    get_inf = local(inf_h, inf_v, 3)
    part = bank_rows // 4
    get_bank = [
        local(bank_h.at[pl.ds(i * part, part)], bank_v.at[pl.ds(i * part, part)], 8 + i) for i in range(4)
    ]
    get_tap = local(tap_h, tap_v, 4)
    get_lab = local(lab_h, lab_v, 5)
    get_outf = local(outf_h, outf_v, 6)
    get_bias = local(bias_h, bias_v, 7)

    def remote(source, target, index, place):
        return pltpu.make_async_remote_copy(
            src_ref=source, dst_ref=target, send_sem=send_sem.at[index], recv_sem=recv_sem.at[index],
            device_id=place, device_id_type=MESH,
        )

    count = jnp.where(head, 0, 3) + jnp.where(tail, 3, 0) + jnp.where(odd, 0, 2)

    @pl.when(count > 0)
    def _():
        pl.semaphore_wait(barrier, count)

    @pl.when(z != 0)
    def _():
        signal(hello.at[1], (lat, prev))
        signal(hello.at[7], (up, prev))
        signal(hello.at[5], (down, prev))

    @pl.when(tail)
    def _():
        signal(hello.at[0], (lat, nxt))
        signal(hello.at[6], (up, nxt))
        signal(hello.at[4], (down, nxt))

    @pl.when(even_lat)
    def _():
        signal(hello.at[3], (up, lon))
        signal(hello.at[2], (down, lon))

    def heard(*indices):
        for index in indices:
            pl.semaphore_wait(hello.at[index], 1)

    get_tr.wait()
    get_slot.wait()
    slots = [slot_s[tr_s[0, 0, j]] for j in range(MAXR)]

    def wanted(owner):
        first = owner * bank_rows
        row_a = row_b = at_a = at_b = count = jnp.int32(0)
        for j in range(MAXR):
            row = slots[j] - first
            hit = (row >= 0) & (row < bank_rows)
            is_a = hit & (count == 0)
            is_b = hit & (count == 1)
            row_a, at_a = jnp.where(is_a, row, row_a), jnp.where(is_a, j, at_a)
            row_b, at_b = jnp.where(is_b, row, row_b), jnp.where(is_b, j, at_b)
            count = count + hit.astype(jnp.int32)
        return row_a, row_b, at_a, at_b

    own_a, own_b, own_at, own_at_b = wanted(lon)
    prev_a, prev_b, prev_at_a, prev_at_b = wanted(prev)
    next_a, next_b, next_at_a, next_at_b = wanted(nxt)
    ask_s[0, 0], ask_s[0, 1] = prev_a, prev_b
    ask_s[1, 0], ask_s[1, 1] = next_a, next_b

    ask_prev = remote(ask_s.at[0], asked_s.at[1], 0, (lat, prev))
    ask_next = remote(ask_s.at[1], asked_s.at[0], 1, (lat, nxt))

    @pl.when(z != 0)
    def _():
        ask_prev.start()

    @pl.when(tail)
    def _():
        ask_next.start()

    get_feat.wait()
    get_inf.wait()
    spread[...] = feat_v[...].astype(F32).reshape(channels * rows, LANES)
    lane = lax.broadcasted_iota(jnp.int32, (rank, LANES), 1)
    packed = jnp.zeros((rank, LANES), F32)
    weights = inf_v[...]
    for r in range(0, rows, 2):
        columns = jnp.concatenate(
            [spread[pl.ds(r + k, channels, stride=rows), :] for k in range(2)], axis=1
        ).astype(BF16)
        pair = dot(weights, columns).astype(BF16)
        red[:, r * LANES : (r + 2) * LANES] = pair
        pair = pair.astype(F32)
        for k in range(2):
            at = 4 * (r + k + REACH)
            rolled = pltpu.roll(pair[:, k * LANES : (k + 1) * LANES], (at + 2) % LANES, 1)
            packed = jnp.where((lane >= at) & (lane < at + 4), rolled, packed)
    pack[...] = packed.astype(BF16)

    edge = REACH * LANES
    whole = rows * LANES
    rims_prev = [
        remote(pack, packs.at[1], 2, (lat, prev)),
        remote(pack, packs.at[5], 6, (up, prev)),
        remote(pack, packs.at[3], 8, (down, prev)),
    ]
    rims_next = [
        remote(pack, packs.at[0], 3, (lat, nxt)),
        remote(pack, packs.at[4], 7, (up, nxt)),
        remote(pack, packs.at[2], 9, (down, nxt)),
    ]
    rims_lat = [
        remote(red.at[:, pl.ds(0, edge)], bots, 4, (up, lon)),
        remote(red.at[:, pl.ds(whole - edge, edge)], tops, 5, (down, lon)),
    ]
    rims = rims_prev + rims_next + rims_lat

    @pl.when(z != 0)
    def _():
        for copy in rims_prev:
            copy.start()

    @pl.when(z != WAVE - 1)
    def _():
        heard(1)
        ask_next.start()
        heard(5, 7)

    for copy in rims_next:
        copy.start()

    @pl.when(odd)
    def _():
        heard(2, 3)

    for copy in rims_lat:
        copy.start()

    give_next = remote(send_cores.at[pl.ds(0, 2)], cores.at[pl.ds(0, 2)], 10, (lat, nxt))
    give_prev = remote(send_cores.at[pl.ds(2, 2)], cores.at[pl.ds(2, 2)], 11, (lat, prev))

    def serve_next():
        ask_prev.wait_recv()
        send_cores[0] = bank_v[asked_s[1, 0]]
        send_cores[1] = bank_v[asked_s[1, 1]]
        give_next.start()

    def serve_prev():
        ask_next.wait_recv()
        send_cores[2] = bank_v[asked_s[0, 0]]
        send_cores[3] = bank_v[asked_s[0, 1]]
        give_prev.start()

    for copy in get_bank:
        copy.wait()
    serve_next()
    pl.when(z != 0)(serve_prev)

    get_tap.wait()
    depth = kron.shape[1]
    taps = tap_v.shape[1]
    pick = (
        lax.broadcasted_iota(jnp.int32, (taps, depth), 1) // rank == lax.broadcasted_iota(jnp.int32, (taps, depth), 0)
    ).astype(F32).astype(BF16)
    wide = dot(tap_v[...], pick)
    same = lax.broadcasted_iota(jnp.int32, (rank, depth), 1) % rank == lax.broadcasted_iota(jnp.int32, (rank, depth), 0)
    for c in range(taps_rank):
        kron[c * rank : (c + 1) * rank, :] = jnp.where(
            same, jnp.broadcast_to(wide[c : c + 1, :], (rank, depth)), 0.0
        ).astype(BF16)

    not_first = (lat > 0).astype(F32)
    not_last = (lat < n_lat - 1).astype(F32)

    def place_row(at, block):
        here = (lane >= 4 * at) & (lane < 4 * at + 4)
        for dx in range(KS):
            rolled = block if dx == REACH else pltpu.roll(block, (REACH - dx) % LANES, 1)
            moved[dx * rank : (dx + 1) * rank, at * LANES : (at + 1) * LANES] = rolled.astype(BF16)
            ends = pltpu.roll(block, (4 * at + 4 - dx) % LANES, 1)
            rim_cells[dx] = jnp.where(here, ends, rim_cells[dx])

    for dx in range(KS):
        rim_cells[dx] = jnp.zeros((rank, LANES), F32)
    for r in range(rows):
        place_row(REACH + r, red[:, r * LANES : (r + 1) * LANES].astype(F32))

    get_lab.wait()
    own_cores = jnp.concatenate([bank_v[own_a], bank_v[own_b]], axis=0)
    span = 2 * LANES
    blank = jnp.zeros((depth - KS * KS * rank, span), BF16)

    def label_row(r):
        return jnp.broadcast_to(lab_v[pl.ds(r, 1), :], (rank, LANES))

    def label_pair(i):
        return jnp.concatenate([label_row(2 * i), label_row(2 * i + 1)], axis=1)

    def tap_rows(i):
        start = pl.multiple_of(i * span, span)
        pieces = [moved[:, pl.ds(pl.multiple_of(start + dy * LANES, LANES), span)] for dy in range(KS)]
        result = dot(kron[...], jnp.concatenate(pieces + [blank], axis=0)).astype(BF16)
        tapped[:, pl.ds(start, span)] = result
        ours = dot(own_cores, result)
        held[:, pl.ds(start, span)] = jnp.where(label_pair(i) == own_at, ours[:rank], ours[rank:])

    pl.loop(1, rows // 2 - 1)(tap_rows)
    for copy in rims_lat:
        copy.wait_recv()
    for r in range(REACH):
        lanes = pl.ds(r * LANES, LANES)
        place_row(r, tops[:, lanes].astype(F32) * not_first)
        place_row(rows + REACH + r, bots[:, lanes].astype(F32) * not_last)
    pl.loop(0, 2)(lambda k: tap_rows(k * (rows // 2 - 1)))

    give_prev.wait_recv()
    next_cores = cores[pl.ds(2, 2)].reshape(2 * rank, cores.shape[2])

    @pl.loop(0, rows // 4, unroll=2)
    def _(i):
        start = pl.multiple_of(i * 2 * span, 2 * span)
        theirs = dot(next_cores, tapped[:, pl.ds(start, 2 * span)])
        label = jnp.concatenate([label_pair(2 * i), label_pair(2 * i + 1)], axis=1)
        hidden = held[:, pl.ds(start, 2 * span)]
        hidden = jnp.where(label == next_at_a, theirs[:rank], hidden)
        held[:, pl.ds(start, 2 * span)] = jnp.where(label == next_at_b, theirs[rank:], hidden)

    get_outf.wait()
    get_bias.wait()
    square = (channels, channels)
    eye = lax.broadcasted_iota(jnp.int32, square, 0) == lax.broadcasted_iota(jnp.int32, square, 1)
    bias = jnp.sum(jnp.where(eye, jnp.broadcast_to(bias_v[...], square), 0.0), axis=1, keepdims=True)
    lab_lane = lax.broadcasted_iota(jnp.int32, (rows, LANES), 1)
    lab_at = 4 * lax.broadcasted_iota(jnp.int32, (rows, LANES), 0)
    lab_rolled = pltpu.roll(lab_v[...], 2, 1, stride=4, stride_axis=0)
    rim_label = jnp.sum(
        jnp.where((lab_lane >= lab_at) & (lab_lane < lab_at + 4), lab_rolled, 0), axis=0, keepdims=True
    )
    rim_label = jnp.broadcast_to(rim_label, (rank, LANES))

    @pl.when(head)
    def _():
        heard(0)
        ask_prev.start()
        heard(4, 6)
        for copy in rims_prev:
            copy.start()
        serve_prev()

    for copy in rims_prev + rims_next:
        copy.wait_recv()
    even = lane % 4 < 2
    middle, above, below = (
        jnp.where(even, packs[2 * k].astype(F32), packs[2 * k + 1].astype(F32)) for k in range(3)
    )
    above = pltpu.roll(above, LANES // 2, 1) * not_first
    below = pltpu.roll(below, LANES // 2, 1) * not_last
    sides = jnp.where(lane < 4 * REACH, above, jnp.where(lane < 4 * (rows + REACH), middle, below))
    spot = lane % 4
    fixed = (
        jnp.where(spot >= 2, pltpu.roll(sides, 2, 1), rim_cells[0]),
        jnp.where(spot == 2, pltpu.roll(sides, 1, 1), rim_cells[1]),
        rim_cells[2],
        jnp.where(spot == 1, pltpu.roll(sides, LANES - 1, 1), rim_cells[3]),
        jnp.where(spot < 2, pltpu.roll(sides, LANES - 2, 1), rim_cells[4]),
    )
    pieces = [
        (pltpu.roll(fixed[dx], LANES - 4 * dy, 1) if dy else fixed[dx]).astype(BF16)
        for dy in range(KS)
        for dx in range(KS)
    ]
    rim_tapped = dot(kron[...], jnp.concatenate(pieces + [blank[:, :LANES]], axis=0)).astype(BF16)
    ready = jnp.concatenate([own_cores, next_cores], axis=0)
    theirs = dot(ready, rim_tapped)
    rim_hidden = theirs[:rank]
    for k, at in enumerate((own_at_b, next_at_a, next_at_b)):
        rim_hidden = jnp.where(rim_label == at, theirs[(k + 1) * rank : (k + 2) * rank], rim_hidden)

    give_next.wait_recv()
    prev_cores = cores[pl.ds(0, 2)].reshape(2 * rank, cores.shape[2])
    last = outf_v[...]
    theirs = dot(prev_cores, rim_tapped)
    rim_hidden = jnp.where(rim_label == prev_at_a, theirs[:rank], rim_hidden)
    rim_hidden = jnp.where(rim_label == prev_at_b, theirs[rank:], rim_hidden)
    at_rim = (lane < REACH) | (lane >= LANES - REACH)
    group = 4
    for first in range(0, rows, group):
        width = group * LANES
        theirs = dot(prev_cores, tapped[:, first * LANES : first * LANES + width])
        parts = []
        for k in range(group):
            r = first + k
            label = label_row(r)
            mine = slice(k * LANES, (k + 1) * LANES)
            hidden = held[:, r * LANES : (r + 1) * LANES]
            hidden = jnp.where(label == prev_at_a, theirs[:rank, mine], hidden)
            hidden = jnp.where(label == prev_at_b, theirs[rank:, mine], hidden)
            beside = pltpu.roll(rim_hidden, (LANES - 2 - 4 * r) % LANES, 1)
            parts.append(jnp.where(at_rim, beside, hidden).astype(BF16))
        value = lax.dot_general(
            last, jnp.concatenate(parts, axis=1), (((0,), (0,)), ((), ())), preferred_element_type=F32
        ) + bias
        value = value / (1.0 + jnp.exp(-value))
        for k in range(group):
            spread[pl.ds(first + k, channels, stride=rows), :] = value[:, k * LANES : (k + 1) * LANES]

    out_ref[...] = spread[...].reshape(channels, rows, LANES).astype(BF16)

    ask_prev.wait_send()
    ask_next.wait_send()
    for copy in rims:
        copy.wait_send()
    give_next.wait_send()
    give_prev.wait_send()


def on_device(features, labels, tile_regions, bank_slot, kernel_bank, in_factor, tap_factor, out_factor, out_bias):
    n_lat, n_lon = lax.axis_size("lat"), lax.axis_size("lon")
    channels, rows, columns = features.shape
    rank = in_factor.shape[0]
    taps_rank, taps = tap_factor.shape
    bank_rows, _, width = kernel_bank.shape
    depth = -(-taps * rank // LANES) * LANES
    cells = rows * columns
    wide = (rows + 2 * REACH) * columns
    dma = pltpu.SemaphoreType.DMA
    anywhere = pl.BlockSpec(memory_space=pltpu.HBM)
    return pl.pallas_call(
        functools.partial(kernel, n_lat, n_lon),
        out_shape=pltpu.VMEM(features.shape, BF16),
        in_specs=[anywhere] * 9,
        out_specs=pl.BlockSpec(memory_space=pltpu.VMEM),
        scratch_shapes=[
            pltpu.VMEM(features.shape, BF16),
            pltpu.VMEM(labels.shape, jnp.int32),
            pltpu.SMEM(tile_regions.shape, jnp.int32),
            pltpu.SMEM(bank_slot.shape, jnp.int32),
            pltpu.VMEM(kernel_bank.shape, BF16),
            pltpu.VMEM(in_factor.shape, BF16),
            pltpu.VMEM(tap_factor.shape, BF16),
            pltpu.VMEM(out_factor.shape[::-1], BF16),
            pltpu.VMEM((1, out_bias.shape[0]), F32),
            pltpu.SMEM((2, 2), jnp.int32),
            pltpu.SMEM((2, 2), jnp.int32),
            pltpu.VMEM((channels * rows, columns), F32),
            pltpu.VMEM((rank, cells), BF16),
            pltpu.VMEM((rank, columns), BF16),
            pltpu.VMEM((6, rank, columns), BF16),
            pltpu.VMEM((rank, REACH * columns), BF16),
            pltpu.VMEM((rank, REACH * columns), BF16),
            pltpu.VMEM((4, rank, width), BF16),
            pltpu.VMEM((4, rank, width), BF16),
            pltpu.VMEM((taps_rank * rank, depth), BF16),
            pltpu.VMEM((KS * rank, wide), BF16),
            pltpu.VMEM((KS, rank, columns), F32),
            pltpu.VMEM((taps_rank * rank, cells), BF16),
            pltpu.VMEM((rank, cells), F32),
            dma((12,)),
            dma((12,)),
            dma((12,)),
            pltpu.SemaphoreType.REGULAR((8,)),
        ],
        compiler_params=pltpu.CompilerParams(
            collective_id=0, has_side_effects=True, vmem_limit_bytes=56 * 1024 * 1024
        ),
        name="layer",
    )(
        features, labels, tile_regions, bank_slot, kernel_bank, in_factor, tap_factor, out_factor.T,
        out_bias.reshape(1, -1),
    )


def solution(mesh):
    placed = (
        P(None, "lat", "lon"),
        P("lat", "lon"),
        P("lat", "lon", None),
        P(),
        P("lon", None, None),
        P(),
        P(),
        P(),
        P(),
    )
    return jax.shard_map(
        on_device, mesh=mesh, in_specs=placed, out_specs=P(None, "lat", "lon"), check_vma=False
    )
```

```python
import functools

import jax
import jax.numpy as jnp
from jax import lax
from jax.experimental import pallas as pl
from jax.experimental.pallas import tpu as pltpu
from jax.sharding import PartitionSpec as P

KS = 5
REACH = KS // 2
LANES = 128
MAXR = 6
WAVE = 12
BF16 = jnp.bfloat16
F32 = jnp.float32
MESH = pl.DeviceIdType.MESH


def dot(a, b):
    return jnp.dot(a, b, preferred_element_type=F32)


def kernel(
    n_lat, n_lon,
    feat_h, lab_h, tr_h, slot_h, bank_h, inf_h, tap_h, outf_h, bias_h,
    out_ref,
    feat_v, lab_v, tr_s, slot_s, bank_v, inf_v, tap_v, outf_v, bias_v,
    ask_s, asked_s, relay_s, spread, red, pack, packs, tops, bots, send_cores, cores,
    kron, moved, rim_cells, tapped, held, local_sem, send_sem, recv_sem, hello,
):
    lat, lon = lax.axis_index("lat"), lax.axis_index("lon")
    up, down = lax.rem(lat + (n_lat - 1), n_lat), lax.rem(lat + 1, n_lat)
    prev, nxt = lax.rem(lon + (n_lon - 1), n_lon), lax.rem(lon + 1, n_lon)
    channels, rows, _ = feat_v.shape
    rank = inf_v.shape[0]
    taps_rank = tap_v.shape[0]
    bank_rows = bank_v.shape[0]
    z = lax.rem(lon, WAVE)
    head, tail, odd = z == 0, z == WAVE - 1, lax.rem(lat, 2) == 1
    even_lat = lax.rem(lat, 2) == 0
    odd_lat = lat + 1 - lax.rem(lat, 2)
    barrier = pltpu.get_barrier_semaphore()

    def signal(semaphore, place):
        pl.semaphore_signal(semaphore, inc=1, device_id=place, device_id_type=MESH)

    @pl.when(z != WAVE - 1)
    def _():
        for line in (lat, up, down):
            signal(barrier, (line, nxt))

    round_trip = lambda steps: lax.rem(lon + steps + n_lon, n_lon)
    head_before, head_after = round_trip(-WAVE), round_trip(WAVE)
    my_tail, my_head = round_trip(WAVE - 1), round_trip(1 - WAVE)

    @pl.when(head)
    def _():
        for line in (lat, up, down):
            signal(barrier, (line, prev))

    relay = head & odd

    @pl.when(relay)
    def _():
        for line in (lat, up):
            signal(barrier, (line, my_tail))
            signal(barrier, (line, head_after))

    @pl.when(odd)
    def _():
        for line in (up, down):
            signal(barrier, (line, lon))

    def local(source, target, index):
        copy = pltpu.make_async_copy(source, target, local_sem.at[index])
        copy.start()
        return copy

    get_tr = local(tr_h, tr_s, 0)
    get_slot = local(slot_h, slot_s, 1)
    get_feat = local(feat_h, feat_v, 2)
    get_inf = local(inf_h, inf_v, 3)
    part = bank_rows // 4
    get_bank = [
        local(bank_h.at[pl.ds(i * part, part)], bank_v.at[pl.ds(i * part, part)], 8 + i) for i in range(4)
    ]
    get_tap = local(tap_h, tap_v, 4)
    get_lab = local(lab_h, lab_v, 5)
    get_outf = local(outf_h, outf_v, 6)
    get_bias = local(bias_h, bias_v, 7)

    def remote(source, target, index, place, lands=None):
        lands = index if lands is None else lands
        return pltpu.make_async_remote_copy(
            src_ref=source, dst_ref=target, send_sem=send_sem.at[index], recv_sem=recv_sem.at[lands],
            device_id=place, device_id_type=MESH,
        )

    count = jnp.where(head, 1, 3) + jnp.where(tail, 4, 0) + jnp.where(odd, 0, 2)

    pl.semaphore_wait(barrier, count)

    @pl.when(tail)
    def _():
        signal(hello.at[8 + lax.rem(lat, 2)], (odd_lat, my_head))
        signal(hello.at[0], (lat, nxt))
        signal(hello.at[6], (up, nxt))
        signal(hello.at[4], (down, nxt))

    @pl.when(z != 0)
    def _():
        signal(hello.at[1], (lat, prev))
        signal(hello.at[7], (up, prev))
        signal(hello.at[5], (down, prev))

    @pl.when(even_lat)
    def _():
        signal(hello.at[3], (up, lon))
        signal(hello.at[2], (down, lon))

    def heard(*indices):
        for index in indices:
            pl.semaphore_wait(hello.at[index], 1)

    get_tr.wait()
    get_slot.wait()
    slots = [slot_s[tr_s[0, 0, j]] for j in range(MAXR)]

    def wanted(owner):
        first = owner * bank_rows
        row_a = row_b = at_a = at_b = count = jnp.int32(0)
        for j in range(MAXR):
            row = slots[j] - first
            hit = (row >= 0) & (row < bank_rows)
            is_a = hit & (count == 0)
            is_b = hit & (count == 1)
            row_a, at_a = jnp.where(is_a, row, row_a), jnp.where(is_a, j, at_a)
            row_b, at_b = jnp.where(is_b, row, row_b), jnp.where(is_b, j, at_b)
            count = count + hit.astype(jnp.int32)
        return row_a, row_b, at_a, at_b

    own_a, own_b, own_at, own_at_b = wanted(lon)
    prev_a, prev_b, prev_at_a, prev_at_b = wanted(prev)
    next_a, next_b, next_at_a, next_at_b = wanted(nxt)
    ask_s[0, 0], ask_s[0, 1] = prev_a, prev_b
    ask_s[1, 0], ask_s[1, 1] = next_a, next_b

    ask_prev = remote(ask_s.at[0], asked_s.at[1], 0, (lat, prev))
    ask_next = remote(ask_s.at[1], asked_s.at[0], 1, (lat, nxt))
    ask_relay = remote(
        ask_s.at[0], relay_s.at[lax.rem(lat, 2)], 12, (odd_lat, head_before), lands=12 + lax.rem(lat, 2)
    )
    relayed = [remote(ask_s.at[0], relay_s.at[k], 12, (odd_lat, head_before), lands=12 + k) for k in range(2)]
    forward = [
        remote(relay_s.at[k], asked_s.at[1], 13 + k, (line, my_tail), lands=0) for k, line in enumerate((up, lat))
    ]

    @pl.when(z != 0)
    def _():
        ask_prev.start()

    @pl.when(tail)
    def _():
        ask_next.start()

    get_feat.wait()
    get_inf.wait()
    spread[...] = feat_v[...].astype(F32).reshape(channels * rows, LANES)
    lane = lax.broadcasted_iota(jnp.int32, (rank, LANES), 1)
    packed = jnp.zeros((rank, LANES), F32)
    weights = inf_v[...]
    for r in range(0, rows, 2):
        columns = jnp.concatenate(
            [spread[pl.ds(r + k, channels, stride=rows), :] for k in range(2)], axis=1
        ).astype(BF16)
        pair = dot(weights, columns).astype(BF16)
        red[:, r * LANES : (r + 2) * LANES] = pair
        pair = pair.astype(F32)
        for k in range(2):
            at = 4 * (r + k + REACH)
            rolled = pltpu.roll(pair[:, k * LANES : (k + 1) * LANES], (at + 2) % LANES, 1)
            packed = jnp.where((lane >= at) & (lane < at + 4), rolled, packed)
    pack[...] = packed.astype(BF16)

    edge = REACH * LANES
    whole = rows * LANES
    rims_prev = [
        remote(pack, packs.at[1], 2, (lat, prev)),
        remote(pack, packs.at[5], 6, (up, prev)),
        remote(pack, packs.at[3], 8, (down, prev)),
    ]
    rims_next = [
        remote(pack, packs.at[0], 3, (lat, nxt)),
        remote(pack, packs.at[4], 7, (up, nxt)),
        remote(pack, packs.at[2], 9, (down, nxt)),
    ]
    rims_lat = [
        remote(red.at[:, pl.ds(0, edge)], bots, 4, (up, lon)),
        remote(red.at[:, pl.ds(whole - edge, edge)], tops, 5, (down, lon)),
    ]
    rims = rims_prev + rims_next + rims_lat

    give_next = remote(send_cores.at[pl.ds(0, 2)], cores.at[pl.ds(0, 2)], 10, (lat, nxt))
    give_prev = remote(send_cores.at[pl.ds(2, 2)], cores.at[pl.ds(2, 2)], 11, (lat, prev))

    def serve_next():
        ask_prev.wait_recv()
        send_cores[0] = bank_v[asked_s[1, 0]]
        send_cores[1] = bank_v[asked_s[1, 1]]
        give_next.start()

    def serve_prev():
        ask_next.wait_recv()
        send_cores[2] = bank_v[asked_s[0, 0]]
        send_cores[3] = bank_v[asked_s[0, 1]]
        give_prev.start()

    def send(copies):
        for copy in copies:
            copy.start()

    @pl.when(tail)
    def _():
        send(rims_next)

    @pl.when(z != 0)
    def _():
        send(rims_prev)

    for copy in get_bank:
        copy.wait()
    pl.when(tail)(serve_next)

    def send_lat():
        pl.when(odd)(lambda: heard(2, 3))
        send(rims_lat)

    pl.when(z != 0)(send_lat)

    @pl.when(z != WAVE - 1)
    def _():
        heard(1)
        ask_next.start()
        heard(5, 7)
        send(rims_next)
        serve_next()

    pl.when(z != 0)(serve_prev)

    pl.when(head)(ask_relay.start)

    get_tap.wait()
    depth = kron.shape[1]
    taps = tap_v.shape[1]
    pick = (
        lax.broadcasted_iota(jnp.int32, (taps, depth), 1) // rank == lax.broadcasted_iota(jnp.int32, (taps, depth), 0)
    ).astype(F32).astype(BF16)
    wide = dot(tap_v[...], pick)
    same = lax.broadcasted_iota(jnp.int32, (rank, depth), 1) % rank == lax.broadcasted_iota(jnp.int32, (rank, depth), 0)
    for c in range(taps_rank):
        kron[c * rank : (c + 1) * rank, :] = jnp.where(
            same, jnp.broadcast_to(wide[c : c + 1, :], (rank, depth)), 0.0
        ).astype(BF16)

    not_first = (lat > 0).astype(F32)
    not_last = (lat < n_lat - 1).astype(F32)

    def place_row(at, block):
        here = (lane >= 4 * at) & (lane < 4 * at + 4)
        for dx in range(KS):
            rolled = block if dx == REACH else pltpu.roll(block, (REACH - dx) % LANES, 1)
            moved[dx * rank : (dx + 1) * rank, at * LANES : (at + 1) * LANES] = rolled.astype(BF16)
            ends = pltpu.roll(block, (4 * at + 4 - dx) % LANES, 1)
            rim_cells[dx] = jnp.where(here, ends, rim_cells[dx])

    for dx in range(KS):
        rim_cells[dx] = jnp.zeros((rank, LANES), F32)
    for r in range(rows):
        place_row(REACH + r, red[:, r * LANES : (r + 1) * LANES].astype(F32))

    get_lab.wait()
    own_cores = jnp.concatenate([bank_v[own_a], bank_v[own_b]], axis=0)
    span = 2 * LANES
    blank = jnp.zeros((depth - KS * KS * rank, span), BF16)

    def label_row(r):
        return jnp.broadcast_to(lab_v[pl.ds(r, 1), :], (rank, LANES))

    def label_pair(i):
        return jnp.concatenate([label_row(2 * i), label_row(2 * i + 1)], axis=1)

    def tap_rows(i):
        start = pl.multiple_of(i * span, span)
        pieces = [moved[:, pl.ds(pl.multiple_of(start + dy * LANES, LANES), span)] for dy in range(KS)]
        result = dot(kron[...], jnp.concatenate(pieces + [blank], axis=0)).astype(BF16)
        tapped[:, pl.ds(start, span)] = result
        ours = dot(own_cores, result)
        held[:, pl.ds(start, span)] = jnp.where(label_pair(i) == own_at, ours[:rank], ours[rank:])

    pl.loop(1, rows // 2 - 1)(tap_rows)
    pl.when(head)(send_lat)

    @pl.when(relay)
    def _():
        for k in (1, 0):
            relayed[k].wait_recv()
            heard(8 + k)
            forward[k].start()

    @pl.when(head)
    def _():
        heard(0, 4, 6)
        send(rims_prev)

    for copy in rims_lat:
        copy.wait_recv()
    for r in range(REACH):
        lanes = pl.ds(r * LANES, LANES)
        place_row(r, tops[:, lanes].astype(F32) * not_first)
        place_row(rows + REACH + r, bots[:, lanes].astype(F32) * not_last)
    pl.loop(0, 2)(lambda k: tap_rows(k * (rows // 2 - 1)))

    give_prev.wait_recv()
    next_cores = cores[pl.ds(2, 2)].reshape(2 * rank, cores.shape[2])

    @pl.loop(0, rows // 4, unroll=2)
    def _(i):
        start = pl.multiple_of(i * 2 * span, 2 * span)
        theirs = dot(next_cores, tapped[:, pl.ds(start, 2 * span)])
        label = jnp.concatenate([label_pair(2 * i), label_pair(2 * i + 1)], axis=1)
        hidden = held[:, pl.ds(start, 2 * span)]
        hidden = jnp.where(label == next_at_a, theirs[:rank], hidden)
        held[:, pl.ds(start, 2 * span)] = jnp.where(label == next_at_b, theirs[rank:], hidden)

    get_outf.wait()
    get_bias.wait()
    square = (channels, channels)
    eye = lax.broadcasted_iota(jnp.int32, square, 0) == lax.broadcasted_iota(jnp.int32, square, 1)
    bias = jnp.sum(jnp.where(eye, jnp.broadcast_to(bias_v[...], square), 0.0), axis=1, keepdims=True)
    lab_lane = lax.broadcasted_iota(jnp.int32, (rows, LANES), 1)
    lab_at = 4 * lax.broadcasted_iota(jnp.int32, (rows, LANES), 0)
    lab_rolled = pltpu.roll(lab_v[...], 2, 1, stride=4, stride_axis=0)
    rim_label = jnp.sum(
        jnp.where((lab_lane >= lab_at) & (lab_lane < lab_at + 4), lab_rolled, 0), axis=0, keepdims=True
    )
    rim_label = jnp.broadcast_to(rim_label, (rank, LANES))

    pl.when(head)(serve_prev)

    for copy in rims_prev + rims_next:
        copy.wait_recv()
    even = lane % 4 < 2
    middle, above, below = (
        jnp.where(even, packs[2 * k].astype(F32), packs[2 * k + 1].astype(F32)) for k in range(3)
    )
    above = pltpu.roll(above, LANES // 2, 1) * not_first
    below = pltpu.roll(below, LANES // 2, 1) * not_last
    sides = jnp.where(lane < 4 * REACH, above, jnp.where(lane < 4 * (rows + REACH), middle, below))
    spot = lane % 4
    fixed = (
        jnp.where(spot >= 2, pltpu.roll(sides, 2, 1), rim_cells[0]),
        jnp.where(spot == 2, pltpu.roll(sides, 1, 1), rim_cells[1]),
        rim_cells[2],
        jnp.where(spot == 1, pltpu.roll(sides, LANES - 1, 1), rim_cells[3]),
        jnp.where(spot < 2, pltpu.roll(sides, LANES - 2, 1), rim_cells[4]),
    )
    pieces = [
        (pltpu.roll(fixed[dx], LANES - 4 * dy, 1) if dy else fixed[dx]).astype(BF16)
        for dy in range(KS)
        for dx in range(KS)
    ]
    rim_tapped = dot(kron[...], jnp.concatenate(pieces + [blank[:, :LANES]], axis=0)).astype(BF16)
    ready = jnp.concatenate([own_cores, next_cores], axis=0)
    theirs = dot(ready, rim_tapped)
    rim_hidden = theirs[:rank]
    for k, at in enumerate((own_at_b, next_at_a, next_at_b)):
        rim_hidden = jnp.where(rim_label == at, theirs[(k + 1) * rank : (k + 2) * rank], rim_hidden)

    give_next.wait_recv()
    prev_cores = cores[pl.ds(0, 2)].reshape(2 * rank, cores.shape[2])
    last = outf_v[...]
    theirs = dot(prev_cores, rim_tapped)
    rim_hidden = jnp.where(rim_label == prev_at_a, theirs[:rank], rim_hidden)
    rim_hidden = jnp.where(rim_label == prev_at_b, theirs[rank:], rim_hidden)
    at_rim = (lane < REACH) | (lane >= LANES - REACH)
    group = 4
    for first in range(0, rows, group):
        width = group * LANES
        theirs = dot(prev_cores, tapped[:, first * LANES : first * LANES + width])
        parts = []
        for k in range(group):
            r = first + k
            label = label_row(r)
            mine = slice(k * LANES, (k + 1) * LANES)
            hidden = held[:, r * LANES : (r + 1) * LANES]
            hidden = jnp.where(label == prev_at_a, theirs[:rank, mine], hidden)
            hidden = jnp.where(label == prev_at_b, theirs[rank:, mine], hidden)
            beside = pltpu.roll(rim_hidden, (LANES - 2 - 4 * r) % LANES, 1)
            parts.append(jnp.where(at_rim, beside, hidden).astype(BF16))
        value = lax.dot_general(
            last, jnp.concatenate(parts, axis=1), (((0,), (0,)), ((), ())), preferred_element_type=F32
        ) + bias
        value = value / (1.0 + jnp.exp(-value))
        for k in range(group):
            spread[pl.ds(first + k, channels, stride=rows), :] = value[:, k * LANES : (k + 1) * LANES]

    out_ref[...] = spread[...].reshape(channels, rows, LANES).astype(BF16)

    pl.when(head)(ask_relay.wait_send)

    @pl.when(relay)
    def _():
        for copy in forward:
            copy.wait_send()

    @pl.when(z != 0)
    def _():
        ask_prev.wait_send()

    ask_next.wait_send()
    for copy in rims:
        copy.wait_send()
    give_next.wait_send()
    give_prev.wait_send()


def on_device(features, labels, tile_regions, bank_slot, kernel_bank, in_factor, tap_factor, out_factor, out_bias):
    n_lat, n_lon = lax.axis_size("lat"), lax.axis_size("lon")
    channels, rows, columns = features.shape
    rank = in_factor.shape[0]
    taps_rank, taps = tap_factor.shape
    bank_rows, _, width = kernel_bank.shape
    depth = -(-taps * rank // LANES) * LANES
    cells = rows * columns
    wide = (rows + 2 * REACH) * columns
    dma = pltpu.SemaphoreType.DMA
    anywhere = pl.BlockSpec(memory_space=pltpu.HBM)
    return pl.pallas_call(
        functools.partial(kernel, n_lat, n_lon),
        out_shape=pltpu.VMEM(features.shape, BF16),
        in_specs=[anywhere] * 9,
        out_specs=pl.BlockSpec(memory_space=pltpu.VMEM),
        scratch_shapes=[
            pltpu.VMEM(features.shape, BF16),
            pltpu.VMEM(labels.shape, jnp.int32),
            pltpu.SMEM(tile_regions.shape, jnp.int32),
            pltpu.SMEM(bank_slot.shape, jnp.int32),
            pltpu.VMEM(kernel_bank.shape, BF16),
            pltpu.VMEM(in_factor.shape, BF16),
            pltpu.VMEM(tap_factor.shape, BF16),
            pltpu.VMEM(out_factor.shape[::-1], BF16),
            pltpu.VMEM((1, out_bias.shape[0]), F32),
            pltpu.SMEM((2, 2), jnp.int32),
            pltpu.SMEM((2, 2), jnp.int32),
            pltpu.SMEM((2, 2), jnp.int32),
            pltpu.VMEM((channels * rows, columns), F32),
            pltpu.VMEM((rank, cells), BF16),
            pltpu.VMEM((rank, columns), BF16),
            pltpu.VMEM((6, rank, columns), BF16),
            pltpu.VMEM((rank, REACH * columns), BF16),
            pltpu.VMEM((rank, REACH * columns), BF16),
            pltpu.VMEM((4, rank, width), BF16),
            pltpu.VMEM((4, rank, width), BF16),
            pltpu.VMEM((taps_rank * rank, depth), BF16),
            pltpu.VMEM((KS * rank, wide), BF16),
            pltpu.VMEM((KS, rank, columns), F32),
            pltpu.VMEM((taps_rank * rank, cells), BF16),
            pltpu.VMEM((rank, cells), F32),
            dma((12,)),
            dma((15,)),
            dma((14,)),
            pltpu.SemaphoreType.REGULAR((10,)),
        ],
        compiler_params=pltpu.CompilerParams(
            collective_id=0, has_side_effects=True, vmem_limit_bytes=56 * 1024 * 1024
        ),
        name="layer",
    )(
        features, labels, tile_regions, bank_slot, kernel_bank, in_factor, tap_factor, out_factor.T,
        out_bias.reshape(1, -1),
    )


def solution(mesh):
    placed = (
        P(None, "lat", "lon"),
        P("lat", "lon"),
        P("lat", "lon", None),
        P(),
        P("lon", None, None),
        P(),
        P(),
        P(),
        P(),
    )
    return jax.shard_map(
        on_device, mesh=mesh, in_specs=placed, out_specs=P(None, "lat", "lon"), check_vma=False
    )
```

```python
import functools

import jax
import jax.numpy as jnp
from jax import lax
from jax.experimental import pallas as pl
from jax.experimental.pallas import tpu as pltpu
from jax.sharding import PartitionSpec as P

KS = 5
REACH = KS // 2
LANES = 128
MAXR = 6
WAVE = 12
BF16 = jnp.bfloat16
F32 = jnp.float32
MESH = pl.DeviceIdType.MESH


def dot(a, b):
    return jnp.dot(a, b, preferred_element_type=F32)


def kernel(
    n_lat, n_lon,
    feat_h, lab_h, tr_h, slot_h, bank_h, inf_h, tap_h, outf_h, bias_h,
    out_ref,
    feat_v, lab_v, tr_s, slot_s, bank_v, inf_v, tap_v, outf_v, bias_v,
    ask_s, asked_s, relay_s, spread, red, pack, packs, tops, bots, send_cores, cores,
    kron, moved, rim_cells, tapped, held, local_sem, send_sem, recv_sem, hello,
):
    lat, lon = lax.axis_index("lat"), lax.axis_index("lon")
    up, down = lax.rem(lat + (n_lat - 1), n_lat), lax.rem(lat + 1, n_lat)
    prev, nxt = lax.rem(lon + (n_lon - 1), n_lon), lax.rem(lon + 1, n_lon)
    channels, rows, _ = feat_v.shape
    rank = inf_v.shape[0]
    taps_rank = tap_v.shape[0]
    bank_rows = bank_v.shape[0]
    z = lax.rem(lon, WAVE)
    head, tail, odd = z == 0, z == WAVE - 1, lax.rem(lat, 2) == 1
    even_lat = lax.rem(lat, 2) == 0
    odd_lat = lat + 1 - lax.rem(lat, 2)
    barrier = pltpu.get_barrier_semaphore()

    def signal(semaphore, place):
        pl.semaphore_signal(semaphore, inc=1, device_id=place, device_id_type=MESH)

    @pl.when(z < WAVE - 2)
    def _():
        for line in (lat, up, down):
            signal(barrier, (line, nxt))

    @pl.when(tail)
    def _():
        for line in (lat, up, down):
            signal(barrier, (line, prev))

    round_trip = lambda steps: lax.rem(lon + steps + n_lon, n_lon)
    head_before, head_after = round_trip(-WAVE), round_trip(WAVE)
    my_tail, my_head = round_trip(WAVE - 1), round_trip(1 - WAVE)

    @pl.when(head)
    def _():
        for line in (lat, up, down):
            signal(barrier, (line, prev))

    relay = head & odd

    @pl.when(relay)
    def _():
        for line in (lat, up):
            signal(barrier, (line, my_tail))
            signal(barrier, (line, head_after))

    @pl.when(odd & (z != WAVE - 1))
    def _():
        for line in (up, down):
            signal(barrier, (line, lon))

    @pl.when(tail)
    def _():
        pl.semaphore_wait(barrier, 4)
        signal(hello.at[8 + lax.rem(lat, 2)], (odd_lat, my_head))
        signal(hello.at[0], (lat, nxt))
        signal(hello.at[6], (up, nxt))
        signal(hello.at[4], (down, nxt))

    def local(source, target, index):
        copy = pltpu.make_async_copy(source, target, local_sem.at[index])
        copy.start()
        return copy

    get_tr = local(tr_h, tr_s, 0)
    get_slot = local(slot_h, slot_s, 1)
    get_feat = local(feat_h, feat_v, 2)
    get_inf = local(inf_h, inf_v, 3)
    part = bank_rows // 4
    get_bank = [
        local(bank_h.at[pl.ds(i * part, part)], bank_v.at[pl.ds(i * part, part)], 8 + i) for i in range(4)
    ]
    get_tap = local(tap_h, tap_v, 4)
    get_lab = local(lab_h, lab_v, 5)
    get_outf = local(outf_h, outf_v, 6)
    get_bias = local(bias_h, bias_v, 7)

    def remote(source, target, index, place, lands=None):
        lands = index if lands is None else lands
        return pltpu.make_async_remote_copy(
            src_ref=source, dst_ref=target, send_sem=send_sem.at[index], recv_sem=recv_sem.at[lands],
            device_id=place, device_id_type=MESH,
        )

    @pl.when(z != WAVE - 1)
    def _():
        before = jnp.where(head, 1, 3) + jnp.where(z == WAVE - 2, 3, 0)
        pl.semaphore_wait(barrier, before + jnp.where(odd, 0, 2))

        @pl.when(even_lat)
        def _():
            signal(hello.at[3], (up, lon))
            signal(hello.at[2], (down, lon))

    @pl.when((z != 0) & (z != WAVE - 1))
    def _():
        signal(hello.at[1], (lat, prev))
        signal(hello.at[7], (up, prev))
        signal(hello.at[5], (down, prev))

    @pl.when(z == WAVE - 2)
    def _():
        signal(hello.at[0], (lat, nxt))
        signal(hello.at[6], (up, nxt))
        signal(hello.at[4], (down, nxt))

    def heard(*indices):
        for index in indices:
            pl.semaphore_wait(hello.at[index], 1)

    get_tr.wait()
    get_slot.wait()
    slots = [slot_s[tr_s[0, 0, j]] for j in range(MAXR)]

    def wanted(owner):
        first = owner * bank_rows
        row_a = row_b = at_a = at_b = count = jnp.int32(0)
        for j in range(MAXR):
            row = slots[j] - first
            hit = (row >= 0) & (row < bank_rows)
            is_a = hit & (count == 0)
            is_b = hit & (count == 1)
            row_a, at_a = jnp.where(is_a, row, row_a), jnp.where(is_a, j, at_a)
            row_b, at_b = jnp.where(is_b, row, row_b), jnp.where(is_b, j, at_b)
            count = count + hit.astype(jnp.int32)
        return row_a, row_b, at_a, at_b

    own_a, own_b, own_at, own_at_b = wanted(lon)
    prev_a, prev_b, prev_at_a, prev_at_b = wanted(prev)
    next_a, next_b, next_at_a, next_at_b = wanted(nxt)
    ask_s[0, 0], ask_s[0, 1] = prev_a, prev_b
    ask_s[1, 0], ask_s[1, 1] = next_a, next_b

    ask_prev = remote(ask_s.at[0], asked_s.at[1], 0, (lat, prev))
    ask_next = remote(ask_s.at[1], asked_s.at[0], 1, (lat, nxt))
    ask_relay = remote(
        ask_s.at[0], relay_s.at[lax.rem(lat, 2)], 12, (odd_lat, head_before), lands=12 + lax.rem(lat, 2)
    )
    relayed = [remote(ask_s.at[0], relay_s.at[k], 12, (odd_lat, head_before), lands=12 + k) for k in range(2)]
    forward = [
        remote(relay_s.at[k], asked_s.at[1], 13 + k, (line, my_tail), lands=0) for k, line in enumerate((up, lat))
    ]

    @pl.when((z != 0) & (z != WAVE - 1))
    def _():
        ask_prev.start()

    @pl.when(tail)
    def _():
        ask_next.start()

    get_feat.wait()
    get_inf.wait()
    spread[...] = feat_v[...].astype(F32).reshape(channels * rows, LANES)
    lane = lax.broadcasted_iota(jnp.int32, (rank, LANES), 1)
    packed = jnp.zeros((rank, LANES), F32)
    weights = inf_v[...]
    for r in range(0, rows, 2):
        columns = jnp.concatenate(
            [spread[pl.ds(r + k, channels, stride=rows), :] for k in range(2)], axis=1
        ).astype(BF16)
        pair = dot(weights, columns).astype(BF16)
        red[:, r * LANES : (r + 2) * LANES] = pair
        pair = pair.astype(F32)
        for k in range(2):
            at = 4 * (r + k + REACH)
            rolled = pltpu.roll(pair[:, k * LANES : (k + 1) * LANES], (at + 2) % LANES, 1)
            packed = jnp.where((lane >= at) & (lane < at + 4), rolled, packed)
    pack[...] = packed.astype(BF16)

    edge = REACH * LANES
    whole = rows * LANES
    rims_prev = [
        remote(pack, packs.at[1], 2, (lat, prev)),
        remote(pack, packs.at[5], 6, (up, prev)),
        remote(pack, packs.at[3], 8, (down, prev)),
    ]
    rims_next = [
        remote(pack, packs.at[0], 3, (lat, nxt)),
        remote(pack, packs.at[4], 7, (up, nxt)),
        remote(pack, packs.at[2], 9, (down, nxt)),
    ]
    rims_lat = [
        remote(red.at[:, pl.ds(0, edge)], bots, 4, (up, lon)),
        remote(red.at[:, pl.ds(whole - edge, edge)], tops, 5, (down, lon)),
    ]
    rims = rims_prev + rims_next + rims_lat

    give_next = remote(send_cores.at[pl.ds(0, 2)], cores.at[pl.ds(0, 2)], 10, (lat, nxt))
    give_prev = remote(send_cores.at[pl.ds(2, 2)], cores.at[pl.ds(2, 2)], 11, (lat, prev))

    def serve_next():
        ask_prev.wait_recv()
        send_cores[0] = bank_v[asked_s[1, 0]]
        send_cores[1] = bank_v[asked_s[1, 1]]
        give_next.start()

    def serve_prev():
        ask_next.wait_recv()
        send_cores[2] = bank_v[asked_s[0, 0]]
        send_cores[3] = bank_v[asked_s[0, 1]]
        give_prev.start()

    def send(copies):
        for copy in copies:
            copy.start()

    @pl.when(tail)
    def _():
        send(rims_next)

    @pl.when((z != 0) & (z != WAVE - 1))
    def _():
        send(rims_prev)

    for copy in get_bank:
        copy.wait()

    @pl.when(tail)
    def _():
        serve_next()
        heard(0)
        ask_prev.start()
        heard(4, 6)
        send(rims_prev)

    def send_lat():
        pl.when(odd & (z != WAVE - 1))(lambda: heard(2, 3))
        send(rims_lat)

    pl.when((z != 0) | even_lat)(send_lat)

    @pl.when(z != WAVE - 1)
    def _():
        pl.when(z != WAVE - 2)(lambda: heard(1))
        ask_next.start()
        pl.when(z != WAVE - 2)(lambda: heard(5, 7))
        send(rims_next)
        serve_next()

    pl.when(z != 0)(serve_prev)

    pl.when(head)(ask_relay.start)

    get_tap.wait()
    depth = kron.shape[1]
    taps = tap_v.shape[1]
    pick = (
        lax.broadcasted_iota(jnp.int32, (taps, depth), 1) // rank == lax.broadcasted_iota(jnp.int32, (taps, depth), 0)
    ).astype(F32).astype(BF16)
    wide = dot(tap_v[...], pick)
    same = lax.broadcasted_iota(jnp.int32, (rank, depth), 1) % rank == lax.broadcasted_iota(jnp.int32, (rank, depth), 0)
    for c in range(taps_rank):
        kron[c * rank : (c + 1) * rank, :] = jnp.where(
            same, jnp.broadcast_to(wide[c : c + 1, :], (rank, depth)), 0.0
        ).astype(BF16)

    not_first = (lat > 0).astype(F32)
    not_last = (lat < n_lat - 1).astype(F32)

    def place_row(at, block):
        here = (lane >= 4 * at) & (lane < 4 * at + 4)
        for dx in range(KS):
            rolled = block if dx == REACH else pltpu.roll(block, (REACH - dx) % LANES, 1)
            moved[dx * rank : (dx + 1) * rank, at * LANES : (at + 1) * LANES] = rolled.astype(BF16)
            ends = pltpu.roll(block, (4 * at + 4 - dx) % LANES, 1)
            rim_cells[dx] = jnp.where(here, ends, rim_cells[dx])

    for dx in range(KS):
        rim_cells[dx] = jnp.zeros((rank, LANES), F32)
    for r in range(rows):
        place_row(REACH + r, red[:, r * LANES : (r + 1) * LANES].astype(F32))

    get_lab.wait()
    own_cores = jnp.concatenate([bank_v[own_a], bank_v[own_b]], axis=0)
    span = 2 * LANES
    blank = jnp.zeros((depth - KS * KS * rank, span), BF16)

    def label_row(r):
        return jnp.broadcast_to(lab_v[pl.ds(r, 1), :], (rank, LANES))

    def label_pair(i):
        return jnp.concatenate([label_row(2 * i), label_row(2 * i + 1)], axis=1)

    def tap_rows(i):
        start = pl.multiple_of(i * span, span)
        pieces = [moved[:, pl.ds(pl.multiple_of(start + dy * LANES, LANES), span)] for dy in range(KS)]
        result = dot(kron[...], jnp.concatenate(pieces + [blank], axis=0)).astype(BF16)
        tapped[:, pl.ds(start, span)] = result
        ours = dot(own_cores, result)
        held[:, pl.ds(start, span)] = jnp.where(label_pair(i) == own_at, ours[:rank], ours[rank:])

    pl.loop(1, rows // 2 - 1)(tap_rows)
    pl.when(relay)(send_lat)

    @pl.when(relay)
    def _():
        for k in (1, 0):
            relayed[k].wait_recv()
            heard(8 + k)
            forward[k].start()

    @pl.when(head)
    def _():
        heard(0, 4, 6)
        send(rims_prev)

    for copy in rims_lat:
        copy.wait_recv()
    for r in range(REACH):
        lanes = pl.ds(r * LANES, LANES)
        place_row(r, tops[:, lanes].astype(F32) * not_first)
        place_row(rows + REACH + r, bots[:, lanes].astype(F32) * not_last)
    pl.loop(0, 2)(lambda k: tap_rows(k * (rows // 2 - 1)))

    give_prev.wait_recv()
    next_cores = cores[pl.ds(2, 2)].reshape(2 * rank, cores.shape[2])

    @pl.loop(0, rows // 4, unroll=2)
    def _(i):
        start = pl.multiple_of(i * 2 * span, 2 * span)
        theirs = dot(next_cores, tapped[:, pl.ds(start, 2 * span)])
        label = jnp.concatenate([label_pair(2 * i), label_pair(2 * i + 1)], axis=1)
        hidden = held[:, pl.ds(start, 2 * span)]
        hidden = jnp.where(label == next_at_a, theirs[:rank], hidden)
        held[:, pl.ds(start, 2 * span)] = jnp.where(label == next_at_b, theirs[rank:], hidden)

    get_outf.wait()
    get_bias.wait()
    square = (channels, channels)
    eye = lax.broadcasted_iota(jnp.int32, square, 0) == lax.broadcasted_iota(jnp.int32, square, 1)
    bias = jnp.sum(jnp.where(eye, jnp.broadcast_to(bias_v[...], square), 0.0), axis=1, keepdims=True)
    lab_lane = lax.broadcasted_iota(jnp.int32, (rows, LANES), 1)
    lab_at = 4 * lax.broadcasted_iota(jnp.int32, (rows, LANES), 0)
    lab_rolled = pltpu.roll(lab_v[...], 2, 1, stride=4, stride_axis=0)
    rim_label = jnp.sum(
        jnp.where((lab_lane >= lab_at) & (lab_lane < lab_at + 4), lab_rolled, 0), axis=0, keepdims=True
    )
    rim_label = jnp.broadcast_to(rim_label, (rank, LANES))

    pl.when(head)(serve_prev)

    for copy in rims_prev + rims_next:
        copy.wait_recv()
    even = lane % 4 < 2
    middle, above, below = (
        jnp.where(even, packs[2 * k].astype(F32), packs[2 * k + 1].astype(F32)) for k in range(3)
    )
    above = pltpu.roll(above, LANES // 2, 1) * not_first
    below = pltpu.roll(below, LANES // 2, 1) * not_last
    sides = jnp.where(lane < 4 * REACH, above, jnp.where(lane < 4 * (rows + REACH), middle, below))
    spot = lane % 4
    fixed = (
        jnp.where(spot >= 2, pltpu.roll(sides, 2, 1), rim_cells[0]),
        jnp.where(spot == 2, pltpu.roll(sides, 1, 1), rim_cells[1]),
        rim_cells[2],
        jnp.where(spot == 1, pltpu.roll(sides, LANES - 1, 1), rim_cells[3]),
        jnp.where(spot < 2, pltpu.roll(sides, LANES - 2, 1), rim_cells[4]),
    )
    pieces = [
        (pltpu.roll(fixed[dx], LANES - 4 * dy, 1) if dy else fixed[dx]).astype(BF16)
        for dy in range(KS)
        for dx in range(KS)
    ]
    rim_tapped = dot(kron[...], jnp.concatenate(pieces + [blank[:, :LANES]], axis=0)).astype(BF16)
    ready = jnp.concatenate([own_cores, next_cores], axis=0)
    theirs = dot(ready, rim_tapped)
    rim_hidden = theirs[:rank]
    for k, at in enumerate((own_at_b, next_at_a, next_at_b)):
        rim_hidden = jnp.where(rim_label == at, theirs[(k + 1) * rank : (k + 2) * rank], rim_hidden)

    give_next.wait_recv()
    prev_cores = cores[pl.ds(0, 2)].reshape(2 * rank, cores.shape[2])
    last = outf_v[...]
    theirs = dot(prev_cores, rim_tapped)
    rim_hidden = jnp.where(rim_label == prev_at_a, theirs[:rank], rim_hidden)
    rim_hidden = jnp.where(rim_label == prev_at_b, theirs[rank:], rim_hidden)
    at_rim = (lane < REACH) | (lane >= LANES - REACH)
    group = 4
    for first in range(0, rows, group):
        width = group * LANES
        theirs = dot(prev_cores, tapped[:, first * LANES : first * LANES + width])
        parts = []
        for k in range(group):
            r = first + k
            label = label_row(r)
            mine = slice(k * LANES, (k + 1) * LANES)
            hidden = held[:, r * LANES : (r + 1) * LANES]
            hidden = jnp.where(label == prev_at_a, theirs[:rank, mine], hidden)
            hidden = jnp.where(label == prev_at_b, theirs[rank:, mine], hidden)
            beside = pltpu.roll(rim_hidden, (LANES - 2 - 4 * r) % LANES, 1)
            parts.append(jnp.where(at_rim, beside, hidden).astype(BF16))
        value = lax.dot_general(
            last, jnp.concatenate(parts, axis=1), (((0,), (0,)), ((), ())), preferred_element_type=F32
        ) + bias
        value = value / (1.0 + jnp.exp(-value))
        for k in range(group):
            spread[pl.ds(first + k, channels, stride=rows), :] = value[:, k * LANES : (k + 1) * LANES]

    out_ref[...] = spread[...].reshape(channels, rows, LANES).astype(BF16)

    pl.when(head)(ask_relay.wait_send)

    @pl.when(relay)
    def _():
        for copy in forward:
            copy.wait_send()

    @pl.when(z != 0)
    def _():
        ask_prev.wait_send()

    ask_next.wait_send()
    for copy in rims:
        copy.wait_send()
    give_next.wait_send()
    give_prev.wait_send()


def on_device(features, labels, tile_regions, bank_slot, kernel_bank, in_factor, tap_factor, out_factor, out_bias):
    n_lat, n_lon = lax.axis_size("lat"), lax.axis_size("lon")
    channels, rows, columns = features.shape
    rank = in_factor.shape[0]
    taps_rank, taps = tap_factor.shape
    bank_rows, _, width = kernel_bank.shape
    depth = -(-taps * rank // LANES) * LANES
    cells = rows * columns
    wide = (rows + 2 * REACH) * columns
    dma = pltpu.SemaphoreType.DMA
    anywhere = pl.BlockSpec(memory_space=pltpu.HBM)
    return pl.pallas_call(
        functools.partial(kernel, n_lat, n_lon),
        out_shape=pltpu.VMEM(features.shape, BF16),
        in_specs=[anywhere] * 9,
        out_specs=pl.BlockSpec(memory_space=pltpu.VMEM),
        scratch_shapes=[
            pltpu.VMEM(features.shape, BF16),
            pltpu.VMEM(labels.shape, jnp.int32),
            pltpu.SMEM(tile_regions.shape, jnp.int32),
            pltpu.SMEM(bank_slot.shape, jnp.int32),
            pltpu.VMEM(kernel_bank.shape, BF16),
            pltpu.VMEM(in_factor.shape, BF16),
            pltpu.VMEM(tap_factor.shape, BF16),
            pltpu.VMEM(out_factor.shape[::-1], BF16),
            pltpu.VMEM((1, out_bias.shape[0]), F32),
            pltpu.SMEM((2, 2), jnp.int32),
            pltpu.SMEM((2, 2), jnp.int32),
            pltpu.SMEM((2, 2), jnp.int32),
            pltpu.VMEM((channels * rows, columns), F32),
            pltpu.VMEM((rank, cells), BF16),
            pltpu.VMEM((rank, columns), BF16),
            pltpu.VMEM((6, rank, columns), BF16),
            pltpu.VMEM((rank, REACH * columns), BF16),
            pltpu.VMEM((rank, REACH * columns), BF16),
            pltpu.VMEM((4, rank, width), BF16),
            pltpu.VMEM((4, rank, width), BF16),
            pltpu.VMEM((taps_rank * rank, depth), BF16),
            pltpu.VMEM((KS * rank, wide), BF16),
            pltpu.VMEM((KS, rank, columns), F32),
            pltpu.VMEM((taps_rank * rank, cells), BF16),
            pltpu.VMEM((rank, cells), F32),
            dma((12,)),
            dma((15,)),
            dma((14,)),
            pltpu.SemaphoreType.REGULAR((10,)),
        ],
        compiler_params=pltpu.CompilerParams(
            collective_id=0, has_side_effects=True, vmem_limit_bytes=56 * 1024 * 1024
        ),
        name="layer",
    )(
        features, labels, tile_regions, bank_slot, kernel_bank, in_factor, tap_factor, out_factor.T,
        out_bias.reshape(1, -1),
    )


def solution(mesh):
    placed = (
        P(None, "lat", "lon"),
        P("lat", "lon"),
        P("lat", "lon", None),
        P(),
        P("lon", None, None),
        P(),
        P(),
        P(),
        P(),
    )
    return jax.shard_map(
        on_device, mesh=mesh, in_specs=placed, out_specs=P(None, "lat", "lon"), check_vma=False
    )
```

```python
import functools

import jax
import jax.numpy as jnp
from jax import lax
from jax.experimental import pallas as pl
from jax.experimental.pallas import tpu as pltpu
from jax.sharding import PartitionSpec as P

KS = 5
REACH = KS // 2
LANES = 128
MAXR = 6
WAVE = 12
BF16 = jnp.bfloat16
F32 = jnp.float32
MESH = pl.DeviceIdType.MESH


def dot(a, b):
    return jnp.dot(a, b, preferred_element_type=F32)


def kernel(
    n_lat, n_lon,
    feat_h, lab_h, tr_h, slot_h, bank_h, inf_h, tap_h, outf_h, bias_h,
    out_ref,
    feat_v, lab_v, tr_s, slot_s, bank_v, inf_v, tap_v, outf_v, bias_v,
    ask_s, asked_s, relay_s, relayed_s, spread, red, pack, packs, tops, bots, send_cores, cores,
    kron, moved, rim_cells, tapped, held, local_sem, send_sem, recv_sem, hello,
):
    lat, lon = lax.axis_index("lat"), lax.axis_index("lon")
    up, down = lax.rem(lat + (n_lat - 1), n_lat), lax.rem(lat + 1, n_lat)
    prev, nxt = lax.rem(lon + (n_lon - 1), n_lon), lax.rem(lon + 1, n_lon)
    channels, rows, _ = feat_v.shape
    rank = inf_v.shape[0]
    taps_rank = tap_v.shape[0]
    bank_rows = bank_v.shape[0]
    z = lax.rem(lon, WAVE)
    head, tail, odd = z == 0, z == WAVE - 1, lax.rem(lat, 2) == 1
    even_lat = lax.rem(lat, 2) == 0
    odd_lat = lat + 1 - lax.rem(lat, 2)
    barrier = pltpu.get_barrier_semaphore()

    def signal(semaphore, place):
        pl.semaphore_signal(semaphore, inc=1, device_id=place, device_id_type=MESH)

    second, middle = z == 1, (z >= 2) & (z <= WAVE - 2)

    @pl.when((z >= 1) & (z < WAVE - 2))
    def _():
        for line in (lat, up, down):
            signal(barrier, (line, nxt))

    @pl.when(tail | second)
    def _():
        for line in (lat, up, down):
            signal(barrier, (line, prev))

    round_trip = lambda steps: lax.rem(lon + steps + n_lon, n_lon)
    head_before, head_after = round_trip(-WAVE), round_trip(WAVE)
    my_tail, my_head = round_trip(WAVE - 1), round_trip(1 - WAVE)

    @pl.when(head)
    def _():
        for line in (lat, up, down):
            signal(barrier, (line, prev))

    relay = head & odd

    @pl.when(relay)
    def _():
        signal(barrier, (lat, my_tail))
        for line in (lat, up):
            signal(barrier, (line, head_after))

    @pl.when(odd & (z != WAVE - 1))
    def _():
        for line in (up, down):
            signal(barrier, (line, lon))

    @pl.when(tail)
    def _():
        pl.semaphore_wait(barrier, jnp.where(odd, 4, 3))
        pl.when(odd)(lambda: signal(hello.at[8], (lat, my_head)))
        signal(hello.at[0], (lat, nxt))
        signal(hello.at[6], (up, nxt))
        signal(hello.at[4], (down, nxt))

    def local(source, target, index):
        copy = pltpu.make_async_copy(source, target, local_sem.at[index])
        copy.start()
        return copy

    get_tr = local(tr_h, tr_s, 0)
    get_slot = local(slot_h, slot_s, 1)
    get_feat = local(feat_h, feat_v, 2)
    get_inf = local(inf_h, inf_v, 3)
    part = bank_rows // 4
    get_bank = [
        local(bank_h.at[pl.ds(i * part, part)], bank_v.at[pl.ds(i * part, part)], 8 + i) for i in range(4)
    ]
    get_tap = local(tap_h, tap_v, 4)
    get_lab = local(lab_h, lab_v, 5)
    get_outf = local(outf_h, outf_v, 6)
    get_bias = local(bias_h, bias_v, 7)

    def remote(source, target, index, place, lands=None):
        lands = index if lands is None else lands
        return pltpu.make_async_remote_copy(
            src_ref=source, dst_ref=target, send_sem=send_sem.at[index], recv_sem=recv_sem.at[lands],
            device_id=place, device_id_type=MESH,
        )

    count = jnp.where(head, 4, jnp.where(second, 0, 3)) + jnp.where(z == WAVE - 2, 3, 0) + jnp.where(odd, 0, 2)

    @pl.when((z != WAVE - 1) & (count > 0))
    def _():
        pl.semaphore_wait(barrier, count)

    @pl.when(even_lat & (z != WAVE - 1))
    def _():
        signal(hello.at[3], (up, lon))
        signal(hello.at[2], (down, lon))

    @pl.when(middle)
    def _():
        signal(hello.at[1], (lat, prev))
        signal(hello.at[7], (up, prev))
        signal(hello.at[5], (down, prev))

    @pl.when(head | (z == WAVE - 2))
    def _():
        signal(hello.at[0], (lat, nxt))
        signal(hello.at[6], (up, nxt))
        signal(hello.at[4], (down, nxt))

    def heard(*indices):
        for index in indices:
            pl.semaphore_wait(hello.at[index], 1)

    get_tr.wait()
    get_slot.wait()
    slots = [slot_s[tr_s[0, 0, j]] for j in range(MAXR)]

    def wanted(owner):
        first = owner * bank_rows
        row_a = row_b = at_a = at_b = count = jnp.int32(0)
        for j in range(MAXR):
            row = slots[j] - first
            hit = (row >= 0) & (row < bank_rows)
            is_a = hit & (count == 0)
            is_b = hit & (count == 1)
            row_a, at_a = jnp.where(is_a, row, row_a), jnp.where(is_a, j, at_a)
            row_b, at_b = jnp.where(is_b, row, row_b), jnp.where(is_b, j, at_b)
            count = count + hit.astype(jnp.int32)
        return row_a, row_b, at_a, at_b

    own_a, own_b, own_at, own_at_b = wanted(lon)
    prev_a, prev_b, prev_at_a, prev_at_b = wanted(prev)
    next_a, next_b, next_at_a, next_at_b = wanted(nxt)
    ask_s[0, 0], ask_s[0, 1] = prev_a, prev_b
    ask_s[1, 0], ask_s[1, 1] = next_a, next_b

    ask_prev = remote(ask_s.at[0], asked_s.at[1], 0, (lat, prev))
    ask_next = remote(ask_s.at[1], asked_s.at[0], 1, (lat, nxt))
    ask_relay = remote(
        ask_s.at[0], relay_s.at[lax.rem(lat, 2)], 12, (odd_lat, head_before), lands=12 + lax.rem(lat, 2)
    )
    relayed = [remote(ask_s.at[0], relay_s.at[k], 12, (odd_lat, head_before), lands=12 + k) for k in range(2)]
    forward = remote(relay_s, relayed_s, 13, (lat, my_tail), lands=14)

    pl.when(middle)(ask_prev.start)

    @pl.when(head)
    def _():
        ask_relay.start()
        ask_next.start()


    @pl.when(tail)
    def _():
        ask_next.start()

    get_feat.wait()
    get_inf.wait()
    spread[...] = feat_v[...].astype(F32).reshape(channels * rows, LANES)
    lane = lax.broadcasted_iota(jnp.int32, (rank, LANES), 1)
    packed = jnp.zeros((rank, LANES), F32)
    weights = inf_v[...]
    for r in range(0, rows, 2):
        columns = jnp.concatenate(
            [spread[pl.ds(r + k, channels, stride=rows), :] for k in range(2)], axis=1
        ).astype(BF16)
        pair = dot(weights, columns).astype(BF16)
        red[:, r * LANES : (r + 2) * LANES] = pair
        pair = pair.astype(F32)
        for k in range(2):
            at = 4 * (r + k + REACH)
            rolled = pltpu.roll(pair[:, k * LANES : (k + 1) * LANES], (at + 2) % LANES, 1)
            packed = jnp.where((lane >= at) & (lane < at + 4), rolled, packed)
    pack[...] = packed.astype(BF16)

    edge = REACH * LANES
    whole = rows * LANES
    rims_prev = [
        remote(pack, packs.at[1], 2, (lat, prev)),
        remote(pack, packs.at[5], 6, (up, prev)),
        remote(pack, packs.at[3], 8, (down, prev)),
    ]
    rims_next = [
        remote(pack, packs.at[0], 3, (lat, nxt)),
        remote(pack, packs.at[4], 7, (up, nxt)),
        remote(pack, packs.at[2], 9, (down, nxt)),
    ]
    rims_lat = [
        remote(red.at[:, pl.ds(0, edge)], bots, 4, (up, lon)),
        remote(red.at[:, pl.ds(whole - edge, edge)], tops, 5, (down, lon)),
    ]
    rims = rims_prev + rims_next + rims_lat

    give_next = remote(send_cores.at[pl.ds(0, 2)], cores.at[pl.ds(0, 2)], 10, (lat, nxt))
    give_prev = remote(send_cores.at[pl.ds(2, 2)], cores.at[pl.ds(2, 2)], 11, (lat, prev))

    def serve_next():
        ask_prev.wait_recv()
        send_cores[0] = bank_v[asked_s[1, 0]]
        send_cores[1] = bank_v[asked_s[1, 1]]
        give_next.start()

    give_pair = remote(send_cores.at[pl.ds(4, 2)], cores.at[pl.ds(0, 2)], 14, (up, nxt), lands=10)

    def serve_heads():
        forward.wait_recv()
        send_cores[0] = bank_v[relayed_s[1, 0]]
        send_cores[1] = bank_v[relayed_s[1, 1]]
        give_next.start()
        send_cores[4] = bank_v[relayed_s[0, 0]]
        send_cores[5] = bank_v[relayed_s[0, 1]]
        give_pair.start()

    def serve_prev():
        ask_next.wait_recv()
        send_cores[2] = bank_v[asked_s[0, 0]]
        send_cores[3] = bank_v[asked_s[0, 1]]
        give_prev.start()

    def send(copies):
        for copy in copies:
            copy.start()

    @pl.when(head | tail)
    def _():
        send(rims_next)

    @pl.when(middle)
    def _():
        send(rims_prev)

    for copy in get_bank:
        copy.wait()

    def greet_prev():
        heard(0)
        ask_prev.start()
        heard(4, 6)
        send(rims_prev)

    @pl.when(tail)
    def _():
        pl.when(odd)(serve_heads)
        greet_prev()

    def send_lat():
        pl.when(odd & (z != WAVE - 1))(lambda: heard(2, 3))
        send(rims_lat)

    pl.when((z != 0) | even_lat)(send_lat)

    @pl.when(second | middle)
    def _():
        pl.when(z != WAVE - 2)(lambda: heard(1))
        ask_next.start()
        pl.when(z != WAVE - 2)(lambda: heard(5, 7))
        send(rims_next)
        serve_next()

    pl.when(z >= 2)(serve_prev)

    get_tap.wait()
    depth = kron.shape[1]
    taps = tap_v.shape[1]
    pick = (
        lax.broadcasted_iota(jnp.int32, (taps, depth), 1) // rank == lax.broadcasted_iota(jnp.int32, (taps, depth), 0)
    ).astype(F32).astype(BF16)
    wide = dot(tap_v[...], pick)
    same = lax.broadcasted_iota(jnp.int32, (rank, depth), 1) % rank == lax.broadcasted_iota(jnp.int32, (rank, depth), 0)
    for c in range(taps_rank):
        kron[c * rank : (c + 1) * rank, :] = jnp.where(
            same, jnp.broadcast_to(wide[c : c + 1, :], (rank, depth)), 0.0
        ).astype(BF16)

    not_first = (lat > 0).astype(F32)
    not_last = (lat < n_lat - 1).astype(F32)

    def place_row(at, block):
        here = (lane >= 4 * at) & (lane < 4 * at + 4)
        for dx in range(KS):
            rolled = block if dx == REACH else pltpu.roll(block, (REACH - dx) % LANES, 1)
            moved[dx * rank : (dx + 1) * rank, at * LANES : (at + 1) * LANES] = rolled.astype(BF16)
            ends = pltpu.roll(block, (4 * at + 4 - dx) % LANES, 1)
            rim_cells[dx] = jnp.where(here, ends, rim_cells[dx])

    for dx in range(KS):
        rim_cells[dx] = jnp.zeros((rank, LANES), F32)
    for r in range(rows):
        place_row(REACH + r, red[:, r * LANES : (r + 1) * LANES].astype(F32))

    get_lab.wait()
    own_cores = jnp.concatenate([bank_v[own_a], bank_v[own_b]], axis=0)
    span = 2 * LANES
    blank = jnp.zeros((depth - KS * KS * rank, span), BF16)

    def label_row(r):
        return jnp.broadcast_to(lab_v[pl.ds(r, 1), :], (rank, LANES))

    def label_pair(i):
        return jnp.concatenate([label_row(2 * i), label_row(2 * i + 1)], axis=1)

    def tap_rows(i):
        start = pl.multiple_of(i * span, span)
        pieces = [moved[:, pl.ds(pl.multiple_of(start + dy * LANES, LANES), span)] for dy in range(KS)]
        result = dot(kron[...], jnp.concatenate(pieces + [blank], axis=0)).astype(BF16)
        tapped[:, pl.ds(start, span)] = result
        ours = dot(own_cores, result)
        held[:, pl.ds(start, span)] = jnp.where(label_pair(i) == own_at, ours[:rank], ours[rank:])

    pl.loop(1, rows // 2 - 1)(tap_rows)
    pl.when(relay)(send_lat)

    @pl.when(second)
    def _():
        greet_prev()
        serve_prev()

    @pl.when(relay)
    def _():
        for copy in relayed:
            copy.wait_recv()
        heard(8)
        forward.start()

    @pl.when(head)
    def _():
        serve_next()
        heard(0, 4, 6)
        send(rims_prev)

    for copy in rims_lat:
        copy.wait_recv()
    for r in range(REACH):
        lanes = pl.ds(r * LANES, LANES)
        place_row(r, tops[:, lanes].astype(F32) * not_first)
        place_row(rows + REACH + r, bots[:, lanes].astype(F32) * not_last)
    pl.loop(0, 2)(lambda k: tap_rows(k * (rows // 2 - 1)))

    give_prev.wait_recv()
    next_cores = cores[pl.ds(2, 2)].reshape(2 * rank, cores.shape[2])

    @pl.loop(0, rows // 4, unroll=2)
    def _(i):
        start = pl.multiple_of(i * 2 * span, 2 * span)
        theirs = dot(next_cores, tapped[:, pl.ds(start, 2 * span)])
        label = jnp.concatenate([label_pair(2 * i), label_pair(2 * i + 1)], axis=1)
        hidden = held[:, pl.ds(start, 2 * span)]
        hidden = jnp.where(label == next_at_a, theirs[:rank], hidden)
        held[:, pl.ds(start, 2 * span)] = jnp.where(label == next_at_b, theirs[rank:], hidden)

    get_outf.wait()
    get_bias.wait()
    square = (channels, channels)
    eye = lax.broadcasted_iota(jnp.int32, square, 0) == lax.broadcasted_iota(jnp.int32, square, 1)
    bias = jnp.sum(jnp.where(eye, jnp.broadcast_to(bias_v[...], square), 0.0), axis=1, keepdims=True)
    lab_lane = lax.broadcasted_iota(jnp.int32, (rows, LANES), 1)
    lab_at = 4 * lax.broadcasted_iota(jnp.int32, (rows, LANES), 0)
    lab_rolled = pltpu.roll(lab_v[...], 2, 1, stride=4, stride_axis=0)
    rim_label = jnp.sum(
        jnp.where((lab_lane >= lab_at) & (lab_lane < lab_at + 4), lab_rolled, 0), axis=0, keepdims=True
    )
    rim_label = jnp.broadcast_to(rim_label, (rank, LANES))

    pl.when(head)(serve_prev)

    for copy in rims_prev + rims_next:
        copy.wait_recv()
    even = lane % 4 < 2
    middle, above, below = (
        jnp.where(even, packs[2 * k].astype(F32), packs[2 * k + 1].astype(F32)) for k in range(3)
    )
    above = pltpu.roll(above, LANES // 2, 1) * not_first
    below = pltpu.roll(below, LANES // 2, 1) * not_last
    sides = jnp.where(lane < 4 * REACH, above, jnp.where(lane < 4 * (rows + REACH), middle, below))
    spot = lane % 4
    fixed = (
        jnp.where(spot >= 2, pltpu.roll(sides, 2, 1), rim_cells[0]),
        jnp.where(spot == 2, pltpu.roll(sides, 1, 1), rim_cells[1]),
        rim_cells[2],
        jnp.where(spot == 1, pltpu.roll(sides, LANES - 1, 1), rim_cells[3]),
        jnp.where(spot < 2, pltpu.roll(sides, LANES - 2, 1), rim_cells[4]),
    )
    pieces = [
        (pltpu.roll(fixed[dx], LANES - 4 * dy, 1) if dy else fixed[dx]).astype(BF16)
        for dy in range(KS)
        for dx in range(KS)
    ]
    rim_tapped = dot(kron[...], jnp.concatenate(pieces + [blank[:, :LANES]], axis=0)).astype(BF16)
    ready = jnp.concatenate([own_cores, next_cores], axis=0)
    theirs = dot(ready, rim_tapped)
    rim_hidden = theirs[:rank]
    for k, at in enumerate((own_at_b, next_at_a, next_at_b)):
        rim_hidden = jnp.where(rim_label == at, theirs[(k + 1) * rank : (k + 2) * rank], rim_hidden)

    give_next.wait_recv()
    prev_cores = cores[pl.ds(0, 2)].reshape(2 * rank, cores.shape[2])
    last = outf_v[...]
    theirs = dot(prev_cores, rim_tapped)
    rim_hidden = jnp.where(rim_label == prev_at_a, theirs[:rank], rim_hidden)
    rim_hidden = jnp.where(rim_label == prev_at_b, theirs[rank:], rim_hidden)
    at_rim = (lane < REACH) | (lane >= LANES - REACH)
    group = 4
    for first in range(0, rows, group):
        width = group * LANES
        theirs = dot(prev_cores, tapped[:, first * LANES : first * LANES + width])
        parts = []
        for k in range(group):
            r = first + k
            label = label_row(r)
            mine = slice(k * LANES, (k + 1) * LANES)
            hidden = held[:, r * LANES : (r + 1) * LANES]
            hidden = jnp.where(label == prev_at_a, theirs[:rank, mine], hidden)
            hidden = jnp.where(label == prev_at_b, theirs[rank:, mine], hidden)
            beside = pltpu.roll(rim_hidden, (LANES - 2 - 4 * r) % LANES, 1)
            parts.append(jnp.where(at_rim, beside, hidden).astype(BF16))
        value = lax.dot_general(
            last, jnp.concatenate(parts, axis=1), (((0,), (0,)), ((), ())), preferred_element_type=F32
        ) + bias
        value = value / (1.0 + jnp.exp(-value))
        for k in range(group):
            spread[pl.ds(first + k, channels, stride=rows), :] = value[:, k * LANES : (k + 1) * LANES]

    out_ref[...] = spread[...].reshape(channels, rows, LANES).astype(BF16)

    pl.when(head)(ask_relay.wait_send)

    pl.when(relay)(forward.wait_send)
    pl.when(tail & odd)(give_pair.wait_send)
    pl.when((z != WAVE - 1) | odd)(give_next.wait_send)

    @pl.when(z != 0)
    def _():
        ask_prev.wait_send()

    ask_next.wait_send()
    for copy in rims:
        copy.wait_send()
    give_prev.wait_send()


def on_device(features, labels, tile_regions, bank_slot, kernel_bank, in_factor, tap_factor, out_factor, out_bias):
    n_lat, n_lon = lax.axis_size("lat"), lax.axis_size("lon")
    channels, rows, columns = features.shape
    rank = in_factor.shape[0]
    taps_rank, taps = tap_factor.shape
    bank_rows, _, width = kernel_bank.shape
    depth = -(-taps * rank // LANES) * LANES
    cells = rows * columns
    wide = (rows + 2 * REACH) * columns
    dma = pltpu.SemaphoreType.DMA
    anywhere = pl.BlockSpec(memory_space=pltpu.HBM)
    return pl.pallas_call(
        functools.partial(kernel, n_lat, n_lon),
        out_shape=pltpu.VMEM(features.shape, BF16),
        in_specs=[anywhere] * 9,
        out_specs=pl.BlockSpec(memory_space=pltpu.VMEM),
        scratch_shapes=[
            pltpu.VMEM(features.shape, BF16),
            pltpu.VMEM(labels.shape, jnp.int32),
            pltpu.SMEM(tile_regions.shape, jnp.int32),
            pltpu.SMEM(bank_slot.shape, jnp.int32),
            pltpu.VMEM(kernel_bank.shape, BF16),
            pltpu.VMEM(in_factor.shape, BF16),
            pltpu.VMEM(tap_factor.shape, BF16),
            pltpu.VMEM(out_factor.shape[::-1], BF16),
            pltpu.VMEM((1, out_bias.shape[0]), F32),
            pltpu.SMEM((2, 2), jnp.int32),
            pltpu.SMEM((2, 2), jnp.int32),
            pltpu.SMEM((2, 2), jnp.int32),
            pltpu.SMEM((2, 2), jnp.int32),
            pltpu.VMEM((channels * rows, columns), F32),
            pltpu.VMEM((rank, cells), BF16),
            pltpu.VMEM((rank, columns), BF16),
            pltpu.VMEM((6, rank, columns), BF16),
            pltpu.VMEM((rank, REACH * columns), BF16),
            pltpu.VMEM((rank, REACH * columns), BF16),
            pltpu.VMEM((6, rank, width), BF16),
            pltpu.VMEM((4, rank, width), BF16),
            pltpu.VMEM((taps_rank * rank, depth), BF16),
            pltpu.VMEM((KS * rank, wide), BF16),
            pltpu.VMEM((KS, rank, columns), F32),
            pltpu.VMEM((taps_rank * rank, cells), BF16),
            pltpu.VMEM((rank, cells), F32),
            dma((12,)),
            dma((15,)),
            dma((15,)),
            pltpu.SemaphoreType.REGULAR((9,)),
        ],
        compiler_params=pltpu.CompilerParams(
            collective_id=0, has_side_effects=True, vmem_limit_bytes=56 * 1024 * 1024
        ),
        name="layer",
    )(
        features, labels, tile_regions, bank_slot, kernel_bank, in_factor, tap_factor, out_factor.T,
        out_bias.reshape(1, -1),
    )


def solution(mesh):
    placed = (
        P(None, "lat", "lon"),
        P("lat", "lon"),
        P("lat", "lon", None),
        P(),
        P("lon", None, None),
        P(),
        P(),
        P(),
        P(),
    )
    return jax.shard_map(
        on_device, mesh=mesh, in_specs=placed, out_specs=P(None, "lat", "lon"), check_vma=False
    )
```

```python
import functools

import jax
import jax.numpy as jnp
from jax import lax
from jax.experimental import pallas as pl
from jax.experimental.pallas import tpu as pltpu
from jax.sharding import PartitionSpec as P

KS = 5
REACH = KS // 2
LANES = 128
MAXR = 6
WAVE = 12
BF16 = jnp.bfloat16
F32 = jnp.float32
MESH = pl.DeviceIdType.MESH


def dot(a, b):
    return jnp.dot(a, b, preferred_element_type=F32)


def kernel(
    n_lat, n_lon,
    feat_h, lab_h, tr_h, slot_h, bank_h, inf_h, tap_h, outf_h, bias_h,
    out_ref,
    feat_v, lab_v, tr_s, slot_s, bank_v, inf_v, tap_v, outf_v, bias_v,
    ask_s, asked_s, relay_s, relayed_s, spread, red, pack, packs, tops, bots, send_cores, cores,
    kron, moved, rim_cells, tapped, held, blend, rim_window, local_sem, send_sem, recv_sem, hello,
):
    lat, lon = lax.axis_index("lat"), lax.axis_index("lon")
    up, down = lax.rem(lat + (n_lat - 1), n_lat), lax.rem(lat + 1, n_lat)
    prev, nxt = lax.rem(lon + (n_lon - 1), n_lon), lax.rem(lon + 1, n_lon)
    channels, rows, _ = feat_v.shape
    rank = inf_v.shape[0]
    taps_rank = tap_v.shape[0]
    bank_rows = bank_v.shape[0]
    def local(source, target, index):
        copy = pltpu.make_async_copy(source, target, local_sem.at[index])
        copy.start()
        return copy

    get_feat = local(feat_h, feat_v, 2)
    get_inf = local(inf_h, inf_v, 3)

    z = lax.rem(lon, WAVE)
    head, tail, odd = z == 0, z == WAVE - 1, lax.rem(lat, 2) == 1
    even_lat = lax.rem(lat, 2) == 0
    odd_lat = lat + 1 - lax.rem(lat, 2)
    barrier = pltpu.get_barrier_semaphore()

    def signal(semaphore, place):
        pl.semaphore_signal(semaphore, inc=1, device_id=place, device_id_type=MESH)

    second, middle = z == 1, (z >= 2) & (z <= WAVE - 2)

    round_trip = lambda steps: lax.rem(lon + steps + n_lon, n_lon)
    head_before, head_after = round_trip(-WAVE), round_trip(WAVE)
    my_tail, my_head = round_trip(WAVE - 1), round_trip(1 - WAVE)

    @pl.when(head)
    def _():
        for line in (lat, up, down):
            signal(barrier, (line, prev))

    relay = head & odd

    @pl.when(relay)
    def _():
        signal(barrier, (lat, my_tail))
        for line in (lat, up):
            signal(barrier, (line, head_after))

    @pl.when(tail)
    def _():
        pl.semaphore_wait(barrier, jnp.where(odd, 4, 3))
        pl.when(odd)(lambda: signal(hello.at[8], (lat, my_head)))
        signal(hello.at[0], (lat, nxt))
        signal(hello.at[6], (up, nxt))
        signal(hello.at[4], (down, nxt))

    @pl.when((z >= 1) & (z < WAVE - 2))
    def _():
        for line in (lat, up, down):
            signal(barrier, (line, nxt))

    @pl.when(tail | second)
    def _():
        for line in (lat, up, down):
            signal(barrier, (line, prev))

    @pl.when(odd & (z != WAVE - 1))
    def _():
        for line in (up, down):
            signal(barrier, (line, lon))

    get_tr = local(tr_h, tr_s, 0)
    get_slot = local(slot_h, slot_s, 1)
    part = bank_rows // 4
    get_bank = [
        local(bank_h.at[pl.ds(i * part, part)], bank_v.at[pl.ds(i * part, part)], 8 + i) for i in range(4)
    ]
    get_tap = local(tap_h, tap_v, 4)
    get_lab = local(lab_h, lab_v, 5)
    get_outf = local(outf_h, outf_v, 6)
    get_bias = local(bias_h, bias_v, 7)

    def remote(source, target, index, place, lands=None):
        lands = index if lands is None else lands
        return pltpu.make_async_remote_copy(
            src_ref=source, dst_ref=target, send_sem=send_sem.at[index], recv_sem=recv_sem.at[lands],
            device_id=place, device_id_type=MESH,
        )

    count = jnp.where(head, 4, jnp.where(second, 0, 3)) + jnp.where(z == WAVE - 2, 3, 0) + jnp.where(odd, 0, 2)

    @pl.when((z != WAVE - 1) & (count > 0))
    def _():
        pl.semaphore_wait(barrier, count)

    @pl.when(even_lat & (z != WAVE - 1))
    def _():
        signal(hello.at[3], (up, lon))
        signal(hello.at[2], (down, lon))

    @pl.when(middle)
    def _():
        signal(hello.at[1], (lat, prev))
        signal(hello.at[7], (up, prev))
        signal(hello.at[5], (down, prev))

    @pl.when(head | (z == WAVE - 2))
    def _():
        signal(hello.at[0], (lat, nxt))
        signal(hello.at[6], (up, nxt))
        signal(hello.at[4], (down, nxt))

    def heard(*indices):
        for index in indices:
            pl.semaphore_wait(hello.at[index], 1)

    get_feat.wait()
    get_inf.wait()
    spread[...] = feat_v[...].astype(F32).reshape(channels * rows, LANES)
    lane = lax.broadcasted_iota(jnp.int32, (rank, LANES), 1)
    packed = jnp.zeros((rank, LANES), F32)
    weights = inf_v[...]
    for r in range(0, rows, 2):
        columns = jnp.concatenate(
            [spread[pl.ds(r + k, channels, stride=rows), :] for k in range(2)], axis=1
        ).astype(BF16)
        pair = dot(weights, columns).astype(BF16)
        red[:, r * LANES : (r + 2) * LANES] = pair
        pair = pair.astype(F32)
        for k in range(2):
            at = 4 * (r + k + REACH)
            rolled = pltpu.roll(pair[:, k * LANES : (k + 1) * LANES], (at + 2) % LANES, 1)
            packed = jnp.where((lane >= at) & (lane < at + 4), rolled, packed)
    pack[...] = packed.astype(BF16)

    edge = REACH * LANES
    whole = rows * LANES
    rims_prev = [
        remote(pack, packs.at[1], 2, (lat, prev)),
        remote(pack, packs.at[5], 6, (up, prev)),
        remote(pack, packs.at[3], 8, (down, prev)),
    ]
    rims_next = [
        remote(pack, packs.at[0], 3, (lat, nxt)),
        remote(pack, packs.at[4], 7, (up, nxt)),
        remote(pack, packs.at[2], 9, (down, nxt)),
    ]
    rims_lat = [
        remote(red.at[:, pl.ds(0, edge)], bots, 4, (up, lon)),
        remote(red.at[:, pl.ds(whole - edge, edge)], tops, 5, (down, lon)),
    ]
    rims = rims_prev + rims_next + rims_lat

    def send(copies):
        for copy in copies:
            copy.start()

    @pl.when(head | tail)
    def _():
        send(rims_next)

    get_tr.wait()
    get_slot.wait()
    slots = [slot_s[tr_s[0, 0, j]] for j in range(MAXR)]

    def wanted(owner):
        first = owner * bank_rows
        row_a = row_b = at_a = at_b = count = jnp.int32(0)
        for j in range(MAXR):
            row = slots[j] - first
            hit = (row >= 0) & (row < bank_rows)
            is_a = hit & (count == 0)
            is_b = hit & (count == 1)
            row_a, at_a = jnp.where(is_a, row, row_a), jnp.where(is_a, j, at_a)
            row_b, at_b = jnp.where(is_b, row, row_b), jnp.where(is_b, j, at_b)
            count = count + hit.astype(jnp.int32)
        return row_a, row_b, at_a, at_b

    own_a, own_b, own_at, own_at_b = wanted(lon)
    prev_a, prev_b, prev_at_a, prev_at_b = wanted(prev)
    next_a, next_b, next_at_a, next_at_b = wanted(nxt)
    ask_s[0, 0], ask_s[0, 1] = prev_a, prev_b
    ask_s[1, 0], ask_s[1, 1] = next_a, next_b

    ask_prev = remote(ask_s.at[0], asked_s.at[1], 0, (lat, prev))
    ask_next = remote(ask_s.at[1], asked_s.at[0], 1, (lat, nxt))
    ask_relay = remote(
        ask_s.at[0], relay_s.at[lax.rem(lat, 2)], 12, (odd_lat, head_before), lands=12 + lax.rem(lat, 2)
    )
    relayed = [remote(ask_s.at[0], relay_s.at[k], 12, (odd_lat, head_before), lands=12 + k) for k in range(2)]
    forward = remote(relay_s, relayed_s, 13, (lat, my_tail), lands=14)

    pl.when(middle)(ask_prev.start)

    @pl.when(head)
    def _():
        ask_relay.start()
        ask_next.start()


    @pl.when(tail)
    def _():
        ask_next.start()

    give_next = remote(send_cores.at[pl.ds(0, 2)], cores.at[pl.ds(0, 2)], 10, (lat, nxt))
    give_prev = remote(send_cores.at[pl.ds(2, 2)], cores.at[pl.ds(2, 2)], 11, (lat, prev))

    def serve_next():
        ask_prev.wait_recv()
        send_cores[0] = bank_v[asked_s[1, 0]]
        send_cores[1] = bank_v[asked_s[1, 1]]
        give_next.start()

    give_pair = remote(send_cores.at[pl.ds(4, 2)], cores.at[pl.ds(0, 2)], 14, (up, nxt), lands=10)

    def serve_heads():
        forward.wait_recv()
        send_cores[0] = bank_v[relayed_s[1, 0]]
        send_cores[1] = bank_v[relayed_s[1, 1]]
        give_next.start()
        send_cores[4] = bank_v[relayed_s[0, 0]]
        send_cores[5] = bank_v[relayed_s[0, 1]]
        give_pair.start()

    def serve_prev():
        ask_next.wait_recv()
        send_cores[2] = bank_v[asked_s[0, 0]]
        send_cores[3] = bank_v[asked_s[0, 1]]
        give_prev.start()

    @pl.when(middle)
    def _():
        send(rims_prev)

    for copy in get_bank:
        copy.wait()

    def greet_prev():
        heard(0)
        ask_prev.start()
        heard(4, 6)
        send(rims_prev)

    @pl.when(tail)
    def _():
        pl.when(odd)(serve_heads)
        greet_prev()

    def send_lat():
        pl.when(odd & (z != WAVE - 1))(lambda: heard(2, 3))
        send(rims_lat)

    pl.when((z != 0) | even_lat)(send_lat)

    @pl.when(second | middle)
    def _():
        pl.when(z != WAVE - 2)(lambda: heard(1))
        ask_next.start()
        pl.when(z != WAVE - 2)(lambda: heard(5, 7))
        send(rims_next)
        serve_next()

    pl.when(z >= 2)(serve_prev)

    get_tap.wait()
    depth = kron.shape[1]
    taps = tap_v.shape[1]
    pick = (
        lax.broadcasted_iota(jnp.int32, (taps, depth), 1) // rank == lax.broadcasted_iota(jnp.int32, (taps, depth), 0)
    ).astype(F32).astype(BF16)
    wide = dot(tap_v[...], pick)
    same = lax.broadcasted_iota(jnp.int32, (rank, depth), 1) % rank == lax.broadcasted_iota(jnp.int32, (rank, depth), 0)
    for c in range(taps_rank):
        kron[c * rank : (c + 1) * rank, :] = jnp.where(
            same, jnp.broadcast_to(wide[c : c + 1, :], (rank, depth)), 0.0
        ).astype(BF16)

    not_first = (lat > 0).astype(F32)
    not_last = (lat < n_lat - 1).astype(F32)

    def place_row(at, block):
        here = (lane >= 4 * at) & (lane < 4 * at + 4)
        for dx in range(KS):
            rolled = block if dx == REACH else pltpu.roll(block, (REACH - dx) % LANES, 1)
            moved[dx * rank : (dx + 1) * rank, at * LANES : (at + 1) * LANES] = rolled.astype(BF16)
            ends = pltpu.roll(block, (4 * at + 4 - dx) % LANES, 1)
            rim_cells[dx] = jnp.where(here, ends, rim_cells[dx])

    for dx in range(KS):
        rim_cells[dx] = jnp.zeros((rank, LANES), F32)
    for r in range(rows):
        place_row(REACH + r, red[:, r * LANES : (r + 1) * LANES].astype(F32))

    get_lab.wait()
    own_cores = jnp.concatenate([bank_v[own_a], bank_v[own_b]], axis=0)
    span = 2 * LANES
    blank = jnp.zeros((depth - KS * KS * rank, span), BF16)

    def label_row(r):
        return jnp.broadcast_to(lab_v[pl.ds(r, 1), :], (rank, LANES))

    def label_pair(i):
        return jnp.concatenate([label_row(2 * i), label_row(2 * i + 1)], axis=1)

    def tap_rows(i):
        start = pl.multiple_of(i * span, span)
        pieces = [moved[:, pl.ds(pl.multiple_of(start + dy * LANES, LANES), span)] for dy in range(KS)]
        result = dot(kron[...], jnp.concatenate(pieces + [blank], axis=0)).astype(BF16)
        tapped[:, pl.ds(start, span)] = result
        ours = dot(own_cores, result)
        held[:, pl.ds(start, span)] = jnp.where(label_pair(i) == own_at, ours[:rank], ours[rank:])

    pl.loop(1, rows // 2 - 1)(tap_rows)
    pl.when(relay)(send_lat)

    @pl.when(second)
    def _():
        greet_prev()
        serve_prev()

    @pl.when(relay)
    def _():
        for copy in relayed:
            copy.wait_recv()
        heard(8)
        forward.start()

    @pl.when(head)
    def _():
        serve_next()

    for copy in rims_lat:
        copy.wait_recv()
    for r in range(REACH):
        lanes = pl.ds(r * LANES, LANES)
        place_row(r, tops[:, lanes].astype(F32) * not_first)
        place_row(rows + REACH + r, bots[:, lanes].astype(F32) * not_last)
    pl.loop(0, 2)(lambda k: tap_rows(k * (rows // 2 - 1)))

    give_prev.wait_recv()
    next_cores = cores[pl.ds(2, 2)].reshape(2 * rank, cores.shape[2])

    @pl.loop(0, rows // 4, unroll=2)
    def _(i):
        start = pl.multiple_of(i * 2 * span, 2 * span)
        theirs = dot(next_cores, tapped[:, pl.ds(start, 2 * span)])
        label = jnp.concatenate([label_pair(2 * i), label_pair(2 * i + 1)], axis=1)
        hidden = held[:, pl.ds(start, 2 * span)]
        hidden = jnp.where(label == next_at_a, theirs[:rank], hidden)
        held[:, pl.ds(start, 2 * span)] = jnp.where(label == next_at_b, theirs[rank:], hidden)

    blend[...] = dot(jnp.concatenate([own_cores, next_cores], axis=0), kron[...]).astype(BF16)
    get_outf.wait()
    get_bias.wait()
    square = (channels, channels)
    eye = lax.broadcasted_iota(jnp.int32, square, 0) == lax.broadcasted_iota(jnp.int32, square, 1)
    bias = jnp.sum(jnp.where(eye, jnp.broadcast_to(bias_v[...], square), 0.0), axis=1, keepdims=True)
    lab_lane = lax.broadcasted_iota(jnp.int32, (rows, LANES), 1)
    lab_at = 4 * lax.broadcasted_iota(jnp.int32, (rows, LANES), 0)
    lab_rolled = pltpu.roll(lab_v[...], 2, 1, stride=4, stride_axis=0)
    rim_label = jnp.sum(
        jnp.where((lab_lane >= lab_at) & (lab_lane < lab_at + 4), lab_rolled, 0), axis=0, keepdims=True
    )
    rim_label = jnp.broadcast_to(rim_label, (rank, LANES))

    @pl.when(head)
    def _():
        heard(0, 4, 6)
        send(rims_prev)
        serve_prev()

    for copy in rims_prev + rims_next:
        copy.wait_recv()
    even = lane % 4 < 2
    beside, above, below = (
        jnp.where(even, packs[2 * k].astype(F32), packs[2 * k + 1].astype(F32)) for k in range(3)
    )
    above = pltpu.roll(above, LANES // 2, 1) * not_first
    below = pltpu.roll(below, LANES // 2, 1) * not_last
    sides = jnp.where(lane < 4 * REACH, above, jnp.where(lane < 4 * (rows + REACH), beside, below))
    spot = lane % 4
    fixed = (
        jnp.where(spot >= 2, pltpu.roll(sides, 2, 1), rim_cells[0]),
        jnp.where(spot == 2, pltpu.roll(sides, 1, 1), rim_cells[1]),
        rim_cells[2],
        jnp.where(spot == 1, pltpu.roll(sides, LANES - 1, 1), rim_cells[3]),
        jnp.where(spot < 2, pltpu.roll(sides, LANES - 2, 1), rim_cells[4]),
    )
    pieces = [
        (pltpu.roll(fixed[dx], LANES - 4 * dy, 1) if dy else fixed[dx]).astype(BF16)
        for dy in range(KS)
        for dx in range(KS)
    ]
    rim_window[...] = jnp.concatenate(pieces + [blank[:, :LANES]], axis=0)
    theirs = dot(blend[...], rim_window[...])
    rim_hidden = theirs[:rank]
    for k, at in enumerate((own_at_b, next_at_a, next_at_b)):
        rim_hidden = jnp.where(rim_label == at, theirs[(k + 1) * rank : (k + 2) * rank], rim_hidden)

    give_next.wait_recv()
    prev_cores = cores[pl.ds(0, 2)].reshape(2 * rank, cores.shape[2])
    theirs = dot(dot(prev_cores, kron[...]).astype(BF16), rim_window[...])
    rim_hidden = jnp.where(rim_label == prev_at_a, theirs[:rank], rim_hidden)
    rim_hidden = jnp.where(rim_label == prev_at_b, theirs[rank:], rim_hidden)
    last = outf_v[...]
    at_rim = (lane < REACH) | (lane >= LANES - REACH)
    group = 4
    for first in range(0, rows, group):
        theirs = dot(prev_cores, tapped[:, first * LANES : (first + group) * LANES])
        parts = []
        for k in range(group):
            r = first + k
            label = label_row(r)
            mine = slice(k * LANES, (k + 1) * LANES)
            hidden = jnp.where(label == prev_at_a, theirs[:rank, mine], held[:, r * LANES : (r + 1) * LANES])
            hidden = jnp.where(label == prev_at_b, theirs[rank:, mine], hidden)
            here = pltpu.roll(rim_hidden, (LANES - 2 - 4 * r) % LANES, 1)
            parts.append(jnp.where(at_rim, here, hidden).astype(BF16))
        value = lax.dot_general(
            last, jnp.concatenate(parts, axis=1), (((0,), (0,)), ((), ())), preferred_element_type=F32
        ) + bias
        value = value / (1.0 + jnp.exp(-value))
        for k in range(group):
            spread[pl.ds(first + k, channels, stride=rows), :] = value[:, k * LANES : (k + 1) * LANES]

    out_ref[...] = spread[...].reshape(channels, rows, LANES).astype(BF16)

    pl.when(head)(ask_relay.wait_send)

    pl.when(relay)(forward.wait_send)
    pl.when(tail & odd)(give_pair.wait_send)
    pl.when((z != WAVE - 1) | odd)(give_next.wait_send)

    @pl.when(z != 0)
    def _():
        ask_prev.wait_send()

    ask_next.wait_send()
    for copy in rims:
        copy.wait_send()
    give_prev.wait_send()


def on_device(features, labels, tile_regions, bank_slot, kernel_bank, in_factor, tap_factor, out_factor, out_bias):
    n_lat, n_lon = lax.axis_size("lat"), lax.axis_size("lon")
    channels, rows, columns = features.shape
    rank = in_factor.shape[0]
    taps_rank, taps = tap_factor.shape
    bank_rows, _, width = kernel_bank.shape
    depth = -(-taps * rank // LANES) * LANES
    cells = rows * columns
    wide = (rows + 2 * REACH) * columns
    dma = pltpu.SemaphoreType.DMA
    anywhere = pl.BlockSpec(memory_space=pltpu.HBM)
    return pl.pallas_call(
        functools.partial(kernel, n_lat, n_lon),
        out_shape=pltpu.VMEM(features.shape, BF16),
        in_specs=[anywhere] * 9,
        out_specs=pl.BlockSpec(memory_space=pltpu.VMEM),
        scratch_shapes=[
            pltpu.VMEM(features.shape, BF16),
            pltpu.VMEM(labels.shape, jnp.int32),
            pltpu.SMEM(tile_regions.shape, jnp.int32),
            pltpu.SMEM(bank_slot.shape, jnp.int32),
            pltpu.VMEM(kernel_bank.shape, BF16),
            pltpu.VMEM(in_factor.shape, BF16),
            pltpu.VMEM(tap_factor.shape, BF16),
            pltpu.VMEM(out_factor.shape[::-1], BF16),
            pltpu.VMEM((1, out_bias.shape[0]), F32),
            pltpu.SMEM((2, 2), jnp.int32),
            pltpu.SMEM((2, 2), jnp.int32),
            pltpu.SMEM((2, 2), jnp.int32),
            pltpu.SMEM((2, 2), jnp.int32),
            pltpu.VMEM((channels * rows, columns), F32),
            pltpu.VMEM((rank, cells), BF16),
            pltpu.VMEM((rank, columns), BF16),
            pltpu.VMEM((6, rank, columns), BF16),
            pltpu.VMEM((rank, REACH * columns), BF16),
            pltpu.VMEM((rank, REACH * columns), BF16),
            pltpu.VMEM((6, rank, width), BF16),
            pltpu.VMEM((4, rank, width), BF16),
            pltpu.VMEM((taps_rank * rank, depth), BF16),
            pltpu.VMEM((KS * rank, wide), BF16),
            pltpu.VMEM((KS, rank, columns), F32),
            pltpu.VMEM((taps_rank * rank, cells), BF16),
            pltpu.VMEM((rank, cells), F32),
            pltpu.VMEM((4 * rank, depth), BF16),
            pltpu.VMEM((depth, columns), BF16),
            dma((12,)),
            dma((15,)),
            dma((15,)),
            pltpu.SemaphoreType.REGULAR((9,)),
        ],
        compiler_params=pltpu.CompilerParams(
            collective_id=0, has_side_effects=True, vmem_limit_bytes=56 * 1024 * 1024
        ),
        name="layer",
    )(
        features, labels, tile_regions, bank_slot, kernel_bank, in_factor, tap_factor, out_factor.T,
        out_bias.reshape(1, -1),
    )


def solution(mesh):
    placed = (
        P(None, "lat", "lon"),
        P("lat", "lon"),
        P("lat", "lon", None),
        P(),
        P("lon", None, None),
        P(),
        P(),
        P(),
        P(),
    )
    return jax.shard_map(
        on_device, mesh=mesh, in_specs=placed, out_specs=P(None, "lat", "lon"), check_vma=False
    )
```

```python
import functools

import jax
import jax.numpy as jnp
from jax import lax
from jax.experimental import pallas as pl
from jax.experimental.pallas import tpu as pltpu
from jax.sharding import PartitionSpec as P

KS = 5
REACH = KS // 2
LANES = 128
MAXR = 6
WAVE = 12
BF16 = jnp.bfloat16
F32 = jnp.float32
MESH = pl.DeviceIdType.MESH


def dot(a, b):
    return jnp.dot(a, b, preferred_element_type=F32)


def kernel(
    n_lat, n_lon,
    feat_h, lab_h, tr_h, slot_h, bank_h, inf_h, tap_h, outf_h, bias_h,
    out_ref,
    feat_v, lab_v, tr_s, slot_s, bank_v, inf_v, tap_v, outf_v, bias_v,
    ask_s, asked_s, relay_s, relayed_s, spread, red, pack, packs, tops, bots, send_cores, cores,
    kron, moved, rim_cells, tapped, held, blend, rim_window, local_sem, send_sem, recv_sem, hello,
):
    lat, lon = lax.axis_index("lat"), lax.axis_index("lon")
    up, down = lax.rem(lat + (n_lat - 1), n_lat), lax.rem(lat + 1, n_lat)
    prev, nxt = lax.rem(lon + (n_lon - 1), n_lon), lax.rem(lon + 1, n_lon)
    channels, rows, _ = feat_v.shape
    rank = inf_v.shape[0]
    taps_rank = tap_v.shape[0]
    bank_rows = bank_v.shape[0]
    def local(source, target, index):
        copy = pltpu.make_async_copy(source, target, local_sem.at[index])
        copy.start()
        return copy

    get_feat = local(feat_h, feat_v, 2)
    get_inf = local(inf_h, inf_v, 3)

    z = lax.rem(lon, WAVE)
    head, tail, odd = z == 0, z == WAVE - 1, lax.rem(lat, 2) == 1
    even_lat = lax.rem(lat, 2) == 0
    odd_lat = lat + 1 - lax.rem(lat, 2)
    barrier = pltpu.get_barrier_semaphore()

    def signal(semaphore, place):
        pl.semaphore_signal(semaphore, inc=1, device_id=place, device_id_type=MESH)

    second, middle = z == 1, (z >= 2) & (z <= WAVE - 2)

    round_trip = lambda steps: lax.rem(lon + steps + n_lon, n_lon)
    head_before, head_after = round_trip(-WAVE), round_trip(WAVE)
    my_tail, my_head = round_trip(WAVE - 1), round_trip(1 - WAVE)

    @pl.when(head)
    def _():
        for line in (lat, up, down):
            signal(barrier, (line, prev))

    relay = head & odd

    @pl.when(relay)
    def _():
        signal(barrier, (lat, my_tail))
        for line in (lat, up):
            signal(barrier, (line, head_after))

    @pl.when(tail)
    def _():
        pl.semaphore_wait(barrier, jnp.where(odd, 4, 3))
        pl.when(odd)(lambda: signal(hello.at[8], (lat, my_head)))
        signal(hello.at[0], (lat, nxt))
        signal(hello.at[6], (up, nxt))
        signal(hello.at[4], (down, nxt))

    @pl.when((z >= 1) & (z < WAVE - 2))
    def _():
        for line in (lat, up, down):
            signal(barrier, (line, nxt))

    @pl.when(tail | second)
    def _():
        for line in (lat, up, down):
            signal(barrier, (line, prev))

    @pl.when(odd & (z != WAVE - 1))
    def _():
        for line in (up, down):
            signal(barrier, (line, lon))

    get_tr = local(tr_h, tr_s, 0)
    get_slot = local(slot_h, slot_s, 1)
    part = bank_rows // 4
    get_bank = [
        local(bank_h.at[pl.ds(i * part, part)], bank_v.at[pl.ds(i * part, part)], 8 + i) for i in range(4)
    ]
    get_tap = local(tap_h, tap_v, 4)
    get_lab = local(lab_h, lab_v, 5)
    get_outf = local(outf_h, outf_v, 6)
    get_bias = local(bias_h, bias_v, 7)

    def remote(source, target, index, place, lands=None):
        lands = index if lands is None else lands
        return pltpu.make_async_remote_copy(
            src_ref=source, dst_ref=target, send_sem=send_sem.at[index], recv_sem=recv_sem.at[lands],
            device_id=place, device_id_type=MESH,
        )

    count = jnp.where(head, 4, jnp.where(second, 0, 3)) + jnp.where(z == WAVE - 2, 3, 0) + jnp.where(odd, 0, 2)

    @pl.when((z != WAVE - 1) & (count > 0))
    def _():
        pl.semaphore_wait(barrier, count)

    @pl.when(even_lat & (z != WAVE - 1))
    def _():
        signal(hello.at[3], (up, lon))
        signal(hello.at[2], (down, lon))

    @pl.when(middle)
    def _():
        signal(hello.at[1], (lat, prev))
        signal(hello.at[7], (up, prev))
        signal(hello.at[5], (down, prev))

    @pl.when(head | (z == WAVE - 2))
    def _():
        signal(hello.at[0], (lat, nxt))
        signal(hello.at[6], (up, nxt))
        signal(hello.at[4], (down, nxt))

    def heard(*indices):
        for index in indices:
            pl.semaphore_wait(hello.at[index], 1)

    get_feat.wait()
    get_inf.wait()
    spread[...] = feat_v[...].astype(F32).reshape(channels * rows, LANES)
    lane = lax.broadcasted_iota(jnp.int32, (rank, LANES), 1)
    packed = jnp.zeros((rank, LANES), F32)
    weights = inf_v[...]
    for r in range(0, rows, 2):
        columns = jnp.concatenate(
            [spread[pl.ds(r + k, channels, stride=rows), :] for k in range(2)], axis=1
        ).astype(BF16)
        pair = dot(weights, columns).astype(BF16)
        red[:, r * LANES : (r + 2) * LANES] = pair
        pair = pair.astype(F32)
        for k in range(2):
            at = 4 * (r + k + REACH)
            rolled = pltpu.roll(pair[:, k * LANES : (k + 1) * LANES], (at + 2) % LANES, 1)
            packed = jnp.where((lane >= at) & (lane < at + 4), rolled, packed)
    pack[...] = packed.astype(BF16)

    edge = REACH * LANES
    whole = rows * LANES
    rims_prev = [
        remote(pack, packs.at[1], 2, (lat, prev)),
        remote(pack, packs.at[5], 6, (up, prev)),
        remote(pack, packs.at[3], 8, (down, prev)),
    ]
    rims_next = [
        remote(pack, packs.at[0], 3, (lat, nxt)),
        remote(pack, packs.at[4], 7, (up, nxt)),
        remote(pack, packs.at[2], 9, (down, nxt)),
    ]
    rims_lat = [
        remote(red.at[:, pl.ds(0, edge)], bots, 4, (up, lon)),
        remote(red.at[:, pl.ds(whole - edge, edge)], tops, 5, (down, lon)),
    ]
    rims = rims_prev + rims_next + rims_lat

    def send(copies):
        for copy in copies:
            copy.start()

    @pl.when(head | tail)
    def _():
        send(rims_next)

    get_tr.wait()
    get_slot.wait()
    slots = [slot_s[tr_s[0, 0, j]] for j in range(MAXR)]

    def wanted(owner):
        first = owner * bank_rows
        row_a = row_b = at_a = at_b = count = jnp.int32(0)
        for j in range(MAXR):
            row = slots[j] - first
            hit = (row >= 0) & (row < bank_rows)
            is_a = hit & (count == 0)
            is_b = hit & (count == 1)
            row_a, at_a = jnp.where(is_a, row, row_a), jnp.where(is_a, j, at_a)
            row_b, at_b = jnp.where(is_b, row, row_b), jnp.where(is_b, j, at_b)
            count = count + hit.astype(jnp.int32)
        return row_a, row_b, at_a, at_b

    own_a, own_b, own_at, own_at_b = wanted(lon)
    prev_a, prev_b, prev_at_a, prev_at_b = wanted(prev)
    next_a, next_b, next_at_a, next_at_b = wanted(nxt)
    ask_s[0, 0], ask_s[0, 1] = prev_a, prev_b
    ask_s[1, 0], ask_s[1, 1] = next_a, next_b

    ask_prev = remote(ask_s.at[0], asked_s.at[1], 0, (lat, prev))
    ask_next = remote(ask_s.at[1], asked_s.at[0], 1, (lat, nxt))
    ask_relay = remote(
        ask_s.at[0], relay_s.at[lax.rem(lat, 2)], 12, (odd_lat, head_before), lands=12 + lax.rem(lat, 2)
    )
    relayed = [remote(ask_s.at[0], relay_s.at[k], 12, (odd_lat, head_before), lands=12 + k) for k in range(2)]
    forward = remote(relay_s, relayed_s, 13, (lat, my_tail), lands=14)

    pl.when(middle)(ask_prev.start)

    @pl.when(head)
    def _():
        ask_relay.start()
        ask_next.start()


    @pl.when(tail)
    def _():
        ask_next.start()

    give_next = remote(send_cores.at[pl.ds(0, 2)], cores.at[pl.ds(0, 2)], 10, (lat, nxt))
    give_prev = remote(send_cores.at[pl.ds(2, 2)], cores.at[pl.ds(2, 2)], 11, (lat, prev))

    def serve_next():
        ask_prev.wait_recv()
        send_cores[0] = bank_v[asked_s[1, 0]]
        send_cores[1] = bank_v[asked_s[1, 1]]
        give_next.start()

    give_pair = remote(send_cores.at[pl.ds(4, 2)], cores.at[pl.ds(0, 2)], 14, (up, nxt), lands=10)

    def serve_heads():
        forward.wait_recv()
        send_cores[0] = bank_v[relayed_s[1, 0]]
        send_cores[1] = bank_v[relayed_s[1, 1]]
        give_next.start()
        send_cores[4] = bank_v[relayed_s[0, 0]]
        send_cores[5] = bank_v[relayed_s[0, 1]]
        give_pair.start()

    def serve_prev():
        ask_next.wait_recv()
        send_cores[2] = bank_v[asked_s[0, 0]]
        send_cores[3] = bank_v[asked_s[0, 1]]
        give_prev.start()

    @pl.when(middle)
    def _():
        send(rims_prev)

    for copy in get_bank:
        copy.wait()

    def greet_prev():
        heard(0)
        ask_prev.start()
        heard(4, 6)
        send(rims_prev)

    @pl.when(tail)
    def _():
        pl.when(odd)(serve_heads)
        greet_prev()

    def send_lat():
        pl.when(odd & (z != WAVE - 1))(lambda: heard(2, 3))
        send(rims_lat)

    pl.when((z != 0) | even_lat)(send_lat)

    @pl.when(second | middle)
    def _():
        pl.when(z != WAVE - 2)(lambda: heard(1))
        ask_next.start()
        pl.when(z != WAVE - 2)(lambda: heard(5, 7))
        send(rims_next)
        serve_next()

    pl.when(z >= 2)(serve_prev)

    get_tap.wait()
    depth = kron.shape[1]
    taps = tap_v.shape[1]
    pick = (
        lax.broadcasted_iota(jnp.int32, (taps, depth), 1) // rank == lax.broadcasted_iota(jnp.int32, (taps, depth), 0)
    ).astype(F32).astype(BF16)
    wide = dot(tap_v[...], pick)
    same = lax.broadcasted_iota(jnp.int32, (rank, depth), 1) % rank == lax.broadcasted_iota(jnp.int32, (rank, depth), 0)
    for c in range(taps_rank):
        kron[c * rank : (c + 1) * rank, :] = jnp.where(
            same, jnp.broadcast_to(wide[c : c + 1, :], (rank, depth)), 0.0
        ).astype(BF16)

    not_first = (lat > 0).astype(F32)
    not_last = (lat < n_lat - 1).astype(F32)

    def place_row(at, block):
        here = (lane >= 4 * at) & (lane < 4 * at + 4)
        for dx in range(KS):
            rolled = block if dx == REACH else pltpu.roll(block, (REACH - dx) % LANES, 1)
            moved[dx * rank : (dx + 1) * rank, at * LANES : (at + 1) * LANES] = rolled.astype(BF16)
            ends = pltpu.roll(block, (4 * at + 4 - dx) % LANES, 1)
            rim_cells[dx] = jnp.where(here, ends, rim_cells[dx])

    for dx in range(KS):
        rim_cells[dx] = jnp.zeros((rank, LANES), F32)
    for r in range(rows):
        place_row(REACH + r, red[:, r * LANES : (r + 1) * LANES].astype(F32))

    get_lab.wait()
    own_cores = jnp.concatenate([bank_v[own_a], bank_v[own_b]], axis=0)
    span = 2 * LANES
    blank = jnp.zeros((depth - KS * KS * rank, span), BF16)

    def label_row(r):
        return jnp.broadcast_to(lab_v[pl.ds(r, 1), :], (rank, LANES))

    def label_pair(i):
        return jnp.concatenate([label_row(2 * i), label_row(2 * i + 1)], axis=1)

    def tap_rows(i):
        start = pl.multiple_of(i * span, span)
        pieces = [moved[:, pl.ds(pl.multiple_of(start + dy * LANES, LANES), span)] for dy in range(KS)]
        result = dot(kron[...], jnp.concatenate(pieces + [blank], axis=0)).astype(BF16)
        tapped[:, pl.ds(start, span)] = result
        ours = dot(own_cores, result)
        held[:, pl.ds(start, span)] = jnp.where(label_pair(i) == own_at, ours[:rank], ours[rank:])

    pl.loop(1, rows // 2 - 1)(tap_rows)
    pl.when(relay)(send_lat)

    @pl.when(second)
    def _():
        greet_prev()
        serve_prev()

    @pl.when(relay)
    def _():
        for copy in relayed:
            copy.wait_recv()
        heard(8)
        forward.start()

    @pl.when(head)
    def _():
        serve_next()

    for copy in rims_lat:
        copy.wait_recv()
    for r in range(REACH):
        lanes = pl.ds(r * LANES, LANES)
        place_row(r, tops[:, lanes].astype(F32) * not_first)
        place_row(rows + REACH + r, bots[:, lanes].astype(F32) * not_last)
    pl.loop(0, 2)(lambda k: tap_rows(k * (rows // 2 - 1)))

    give_prev.wait_recv()
    next_cores = cores[pl.ds(2, 2)].reshape(2 * rank, cores.shape[2])

    @pl.loop(0, rows // 4, unroll=2)
    def _(i):
        start = pl.multiple_of(i * 2 * span, 2 * span)
        theirs = dot(next_cores, tapped[:, pl.ds(start, 2 * span)])
        label = jnp.concatenate([label_pair(2 * i), label_pair(2 * i + 1)], axis=1)
        hidden = held[:, pl.ds(start, 2 * span)]
        hidden = jnp.where(label == next_at_a, theirs[:rank], hidden)
        held[:, pl.ds(start, 2 * span)] = jnp.where(label == next_at_b, theirs[rank:], hidden)

    blend[...] = dot(jnp.concatenate([own_cores, next_cores], axis=0), kron[...]).astype(BF16)
    get_outf.wait()
    get_bias.wait()
    square = (channels, channels)
    eye = lax.broadcasted_iota(jnp.int32, square, 0) == lax.broadcasted_iota(jnp.int32, square, 1)
    bias = jnp.sum(jnp.where(eye, jnp.broadcast_to(bias_v[...], square), 0.0), axis=1, keepdims=True)
    lab_lane = lax.broadcasted_iota(jnp.int32, (rows, LANES), 1)
    lab_at = 4 * lax.broadcasted_iota(jnp.int32, (rows, LANES), 0)
    lab_rolled = pltpu.roll(lab_v[...], 2, 1, stride=4, stride_axis=0)
    rim_label = jnp.sum(
        jnp.where((lab_lane >= lab_at) & (lab_lane < lab_at + 4), lab_rolled, 0), axis=0, keepdims=True
    )
    rim_label = jnp.broadcast_to(rim_label, (rank, LANES))

    @pl.when(head)
    def _():
        heard(0, 4, 6)
        send(rims_prev)
        serve_prev()

    for copy in rims_prev + rims_next:
        copy.wait_recv()
    even = lane % 4 < 2
    beside, above, below = (
        jnp.where(even, packs[2 * k].astype(F32), packs[2 * k + 1].astype(F32)) for k in range(3)
    )
    above = pltpu.roll(above, LANES // 2, 1) * not_first
    below = pltpu.roll(below, LANES // 2, 1) * not_last
    sides = jnp.where(lane < 4 * REACH, above, jnp.where(lane < 4 * (rows + REACH), beside, below))
    spot = lane % 4
    fixed = (
        jnp.where(spot >= 2, pltpu.roll(sides, 2, 1), rim_cells[0]),
        jnp.where(spot == 2, pltpu.roll(sides, 1, 1), rim_cells[1]),
        rim_cells[2],
        jnp.where(spot == 1, pltpu.roll(sides, LANES - 1, 1), rim_cells[3]),
        jnp.where(spot < 2, pltpu.roll(sides, LANES - 2, 1), rim_cells[4]),
    )
    pieces = [
        (pltpu.roll(fixed[dx], LANES - 4 * dy, 1) if dy else fixed[dx]).astype(BF16)
        for dy in range(KS)
        for dx in range(KS)
    ]
    rim_window[...] = jnp.concatenate(pieces + [blank[:, :LANES]], axis=0)
    theirs = dot(blend[...], rim_window[...])
    rim_hidden = theirs[:rank]
    for k, at in enumerate((own_at_b, next_at_a, next_at_b)):
        rim_hidden = jnp.where(rim_label == at, theirs[(k + 1) * rank : (k + 2) * rank], rim_hidden)

    give_next.wait_recv()
    prev_cores = cores[pl.ds(0, 2)].reshape(2 * rank, cores.shape[2])
    theirs = dot(dot(prev_cores, kron[...]).astype(BF16), rim_window[...])
    rim_hidden = jnp.where(rim_label == prev_at_a, theirs[:rank], rim_hidden)
    rim_hidden = jnp.where(rim_label == prev_at_b, theirs[rank:], rim_hidden)
    last = outf_v[...]
    at_rim = (lane < REACH) | (lane >= LANES - REACH)
    group = 16
    for first in range(0, rows, group):
        theirs = dot(prev_cores, tapped[:, first * LANES : (first + group) * LANES])
        parts = []
        for k in range(group):
            r = first + k
            label = label_row(r)
            mine = slice(k * LANES, (k + 1) * LANES)
            hidden = jnp.where(label == prev_at_a, theirs[:rank, mine], held[:, r * LANES : (r + 1) * LANES])
            hidden = jnp.where(label == prev_at_b, theirs[rank:, mine], hidden)
            here = pltpu.roll(rim_hidden, (LANES - 2 - 4 * r) % LANES, 1)
            parts.append(jnp.where(at_rim, here, hidden).astype(BF16))
        value = lax.dot_general(
            last, jnp.concatenate(parts, axis=1), (((0,), (0,)), ((), ())), preferred_element_type=F32
        ) + bias
        value = value / (1.0 + jnp.exp(-value))
        for k in range(group):
            spread[pl.ds(first + k, channels, stride=rows), :] = value[:, k * LANES : (k + 1) * LANES]

    out_ref[...] = spread[...].reshape(channels, rows, LANES).astype(BF16)

    pl.when(head)(ask_relay.wait_send)

    pl.when(relay)(forward.wait_send)
    pl.when(tail & odd)(give_pair.wait_send)
    pl.when((z != WAVE - 1) | odd)(give_next.wait_send)

    @pl.when(z != 0)
    def _():
        ask_prev.wait_send()

    ask_next.wait_send()
    for copy in rims:
        copy.wait_send()
    give_prev.wait_send()


def on_device(features, labels, tile_regions, bank_slot, kernel_bank, in_factor, tap_factor, out_factor, out_bias):
    n_lat, n_lon = lax.axis_size("lat"), lax.axis_size("lon")
    channels, rows, columns = features.shape
    rank = in_factor.shape[0]
    taps_rank, taps = tap_factor.shape
    bank_rows, _, width = kernel_bank.shape
    depth = -(-taps * rank // LANES) * LANES
    cells = rows * columns
    wide = (rows + 2 * REACH) * columns
    dma = pltpu.SemaphoreType.DMA
    anywhere = pl.BlockSpec(memory_space=pltpu.HBM)
    return pl.pallas_call(
        functools.partial(kernel, n_lat, n_lon),
        out_shape=pltpu.VMEM(features.shape, BF16),
        in_specs=[anywhere] * 9,
        out_specs=pl.BlockSpec(memory_space=pltpu.VMEM),
        scratch_shapes=[
            pltpu.VMEM(features.shape, BF16),
            pltpu.VMEM(labels.shape, jnp.int32),
            pltpu.SMEM(tile_regions.shape, jnp.int32),
            pltpu.SMEM(bank_slot.shape, jnp.int32),
            pltpu.VMEM(kernel_bank.shape, BF16),
            pltpu.VMEM(in_factor.shape, BF16),
            pltpu.VMEM(tap_factor.shape, BF16),
            pltpu.VMEM(out_factor.shape[::-1], BF16),
            pltpu.VMEM((1, out_bias.shape[0]), F32),
            pltpu.SMEM((2, 2), jnp.int32),
            pltpu.SMEM((2, 2), jnp.int32),
            pltpu.SMEM((2, 2), jnp.int32),
            pltpu.SMEM((2, 2), jnp.int32),
            pltpu.VMEM((channels * rows, columns), F32),
            pltpu.VMEM((rank, cells), BF16),
            pltpu.VMEM((rank, columns), BF16),
            pltpu.VMEM((6, rank, columns), BF16),
            pltpu.VMEM((rank, REACH * columns), BF16),
            pltpu.VMEM((rank, REACH * columns), BF16),
            pltpu.VMEM((6, rank, width), BF16),
            pltpu.VMEM((4, rank, width), BF16),
            pltpu.VMEM((taps_rank * rank, depth), BF16),
            pltpu.VMEM((KS * rank, wide), BF16),
            pltpu.VMEM((KS, rank, columns), F32),
            pltpu.VMEM((taps_rank * rank, cells), BF16),
            pltpu.VMEM((rank, cells), F32),
            pltpu.VMEM((4 * rank, depth), BF16),
            pltpu.VMEM((depth, columns), BF16),
            dma((12,)),
            dma((15,)),
            dma((15,)),
            pltpu.SemaphoreType.REGULAR((9,)),
        ],
        compiler_params=pltpu.CompilerParams(
            collective_id=0, has_side_effects=True, vmem_limit_bytes=56 * 1024 * 1024
        ),
        name="layer",
    )(
        features, labels, tile_regions, bank_slot, kernel_bank, in_factor, tap_factor, out_factor.T,
        out_bias.reshape(1, -1),
    )


def solution(mesh):
    placed = (
        P(None, "lat", "lon"),
        P("lat", "lon"),
        P("lat", "lon", None),
        P(),
        P("lon", None, None),
        P(),
        P(),
        P(),
        P(),
    )
    return jax.shard_map(
        on_device, mesh=mesh, in_specs=placed, out_specs=P(None, "lat", "lon"), check_vma=False
    )
```
